32 devices in a mesh: ctx: 8 (over z, y), head: 4 (over x, core).
Axes of the slice: x: 2, y: 2, z: 4, core: 2. Of those that a mesh axis runs over, the one named last changes fastest.
Arguments:
- signal: bfloat16 [4096, 4096], P('ctx', 'head'), may hold values from -6 to 6
- gate_input: bfloat16 [4096, 4096], P('ctx', 'head'), may hold values from -6 to 6
- input_map: bfloat16 [4096, 1024], P('ctx', 'head'), may hold values from -0.5 to 0.5
- readout: bfloat16 [4096, 1024], P('ctx', 'head'), may hold values from -0.5 to 0.5
- log_decay: float32 [64, 4096], P('head', 'ctx'), may hold values from -1.3 to 0
- skip_gain: float32 [64], P('head'), may hold values from 0.5 to 1.5
- norm_gain: float32 [4096], P('head'), may hold values from 0.5 to 1.5
- out_weight: bfloat16 [4096, 2048], P('head'), may hold values from -0.09375 to 0.09375
- out_grad: bfloat16 [4096, 2048], P(('ctx', 'head')), may hold values from -8 to 8
Outputs:
- layer_out: bfloat16 [4096, 2048], P(('ctx', 'head'))
- signal_grad: float32 [4096, 4096], P('ctx', 'head')
- gate_grad: float32 [4096, 4096], P('ctx', 'head')
- input_map_grad: float32 [4096, 1024], P('ctx', 'head')
- readout_grad: float32 [4096, 1024], P('ctx', 'head')
- decay_grad: float32 [64, 4096], P('head', 'ctx')
- skip_grad: float32 [64], P('head')
- gain_grad: float32 [4096], P('head')
- weight_grad: float32 [4096, 2048], P('head')
The draws below stay inside these ranges and needn't reach their ends.
All inputs are finite; a program needn't handle non-finite values.
Results may differ from the reference program's by a relative error of at most 0.0049.
Values may be sent and summed in bfloat16 or wider, within the bound.
A program may use at most 128 MiB of HBM per device.

```python
import math
from functools import partial
import jax
import jax.numpy as jnp
from jax import lax

D = 2048
HEADS = 64
P_SIZE = 64
N = 128
GROUPS = 8
SPAN = 256
TOKEN_TOTAL = 4096
INNER = 4096


def draw_log_decay(key, part):
    keys = jax.random.split(key, 7)
    slow_share = 0.5
    is_slow = jax.random.bernoulli(keys[0], slow_share, (HEADS, 1))
    slow_rate = jax.random.uniform(keys[1], (HEADS, 1), jnp.float32, 0.1, 0.5) / TOKEN_TOTAL
    fast_rate = jax.random.uniform(keys[2], (HEADS, 1), jnp.float32, 1.0 / 50.0, 1.0 / 30.0)
    reference_speed = jnp.where(is_slow, slow_rate, fast_rate)
    rough_multiplier = jax.random.uniform(keys[3], (HEADS, TOKEN_TOTAL), jnp.float32, 0.5, 1.5)
    block_log = jax.random.uniform(keys[4], (HEADS, TOKEN_TOTAL // SPAN), jnp.float32, math.log(0.5), math.log(2.0))
    tile_multiplier = jnp.repeat(jnp.exp(block_log), SPAN, axis=1)
    location_numbers = jax.random.randint(keys[5], (HEADS, 2, 1), 0, TOKEN_TOTAL)
    quantity_entries = jax.random.uniform(keys[6], (HEADS, 2, 1), jnp.float32, 0.2, 0.6)
    packet_clusters = jnp.sum(jnp.where(jnp.arange(TOKEN_TOTAL)[None, None, :] == location_numbers, quantity_entries, 0.0), axis=1)
    return -(reference_speed * rough_multiplier * tile_multiplier) - packet_clusters


def draw_out_grad(key, part):
    keys = jax.random.split(key, 1)
    ramp_up = 0.5 + 1.5 * jnp.arange(TOKEN_TOTAL, dtype=jnp.float32)[:, None] / TOKEN_TOTAL
    base_val = jax.random.normal(keys[0], (TOKEN_TOTAL, D), jnp.float32)
    return jnp.clip(base_val * ramp_up, -8.0, 8.0).astype(jnp.bfloat16)


def levels(stream_key, extent, shards, smallest, high):
    def one(dim, shards_of):
        draws = jax.random.uniform(jax.random.fold_in(jax.random.fold_in(stream_key, 6), dim), (shards_of,), jnp.float32, smallest / len(shards), high / len(shards))
        return jnp.repeat(jnp.exp(draws), extent[dim] // shards_of).reshape((-1,) + (1,) * (len(extent) - dim - 1))

    loudness = one(*shards[0])
    for cut in shards[1:]:
        loudness = loudness * one(*cut)
    return loudness


def noise(stream_key, shape, spread, bound, cuts=(), kind=jnp.bfloat16):
    drawn = spread * jax.random.normal(stream_key, shape, jnp.float32)
    if cuts:
        drawn = drawn * levels(stream_key, shape, cuts, -0.22, 0.18)
    return jnp.clip(drawn, -bound, bound).astype(kind)


def setup_inputs(seed: int = 0) -> dict:
    splits = jax.random.split(jax.random.key(seed), 10)
    return {
        "signal": noise(splits[0], (TOKEN_TOTAL, INNER), 1.0, 6.0, ((0, 8), (1, 4))),
        "gate_input": noise(splits[1], (TOKEN_TOTAL, INNER), 1.0, 6.0, ((0, 8), (1, 4))),
        "input_map": noise(splits[2], (TOKEN_TOTAL, GROUPS * N), N ** -0.5, 0.5, ((0, 8), (1, 4))),
        "readout": noise(splits[3], (TOKEN_TOTAL, GROUPS * N), N ** -0.5, 0.5, ((0, 8), (1, 4))),
        "log_decay": draw_log_decay(jax.random.fold_in(splits[9], 71), 0),
        "skip_gain": jnp.clip(0.5 + 1.0 * jax.random.uniform(splits[5], (HEADS,), jnp.float32) ** levels(splits[5], (HEADS,), ((0, 4),), -0.2, 0.2), 0.5, 1.5),
        "norm_gain": jnp.clip(0.5 + 1.0 * jax.random.uniform(splits[6], (INNER,), jnp.float32) ** levels(splits[6], (INNER,), ((0, 4),), -0.2, 0.2), 0.5, 1.5),
        "out_weight": noise(splits[7], (INNER, D), INNER ** -0.5, 0.09375, ((0, 4),)),
        "out_grad": draw_out_grad(jax.random.fold_in(splits[9], 71), 0),
    }


contract = partial(jnp.einsum, precision=lax.Precision.HIGHEST)

def span_parts(decay_log, map_f, read_f):
    cumulative = jnp.cumsum(decay_log, axis=-1)
    log_gap = cumulative[..., :, None] - cumulative[..., None, :]
    span_len = decay_log.shape[-1]
    lower_tri = jnp.arange(span_len)[:, None] >= jnp.arange(span_len)[None, :]
    lower_decay = jnp.where(lower_tri, jnp.exp(jnp.minimum(log_gap, 0.0)), 0.0)
    inner_prod = contract('ign,jgn->gij', read_f, map_f)
    mixing = lower_decay * inner_prod[:, None]
    to_closing = jnp.exp(cumulative[..., -1:] - cumulative)
    from_start = jnp.moveaxis(jnp.exp(cumulative), -1, 0)
    return (cumulative, lower_decay, mixing, to_closing, from_start)

def forward_step(carry_state, span_item):
    decay_log, signal_f, map_f, read_f = span_item
    cumulative, lower_decay, mixing, to_closing, from_start = span_parts(decay_log, map_f, read_f)
    core_out = contract('ghij,jghp->ighp', mixing, signal_f)
    core_out = core_out + from_start[..., None] * contract('ghpn,ign->ighp', carry_state, read_f)
    next_state = jnp.exp(cumulative[..., -1])[..., None, None] * carry_state
    next_state = next_state + contract('ghj,jghp,jgn->ghpn', to_closing, signal_f, map_f)
    return (next_state, (core_out, carry_state))

def backward_step(carry_grad, span_item):
    decay_log, signal_f, map_f, read_f, grad_y, core_out, carry_state = span_item
    cumulative, lower_decay, mixing, to_closing, from_start = span_parts(decay_log, map_f, read_f)
    core_grad = contract('ghij,ighp->jghp', mixing, grad_y)
    core_grad = core_grad + contract('ghj,ghpn,jgn->jghp', to_closing, carry_grad, map_f)
    pair_grad = contract('ighp,jghp->ghij', grad_y, signal_f) * lower_decay
    map_grad = contract('ghij,ign->jgn', pair_grad, read_f)
    map_grad = map_grad + contract('ghj,ghpn,jghp->jgn', to_closing, carry_grad, signal_f)
    read_grad = contract('ghij,jgn->ign', pair_grad, map_f)
    read_grad = read_grad + contract('igh,ghpn,ighp->ign', from_start, carry_state, grad_y)
    earlier_grad = jnp.exp(cumulative[..., -1])[..., None, None] * carry_grad
    earlier_grad = earlier_grad + contract('igh,ighp,ign->ghpn', from_start, grad_y, read_f)
    log_slope = lax.optimization_barrier(jnp.sum(grad_y * core_out - signal_f * core_grad, axis=-1))
    return (earlier_grad, (core_grad, map_grad, read_grad, log_slope))

def reference(signal, gate_input, input_map, readout, log_decay, skip_gain, norm_gain, out_weight, out_grad):
    length = signal.shape[0]
    span_count = length // SPAN
    heads_group = HEADS // GROUPS
    group_width = heads_group * P_SIZE
    signal_f = signal.astype(jnp.float32).reshape(span_count, SPAN, GROUPS, heads_group, P_SIZE)
    map_f = input_map.astype(jnp.float32).reshape(span_count, SPAN, GROUPS, N)
    read_f = readout.astype(jnp.float32).reshape(span_count, SPAN, GROUPS, N)
    decay_log = log_decay.reshape(GROUPS, heads_group, span_count, SPAN).transpose(2, 0, 1, 3)
    skip_scale = skip_gain.reshape(GROUPS, heads_group)[:, :, None]
    initial = jnp.zeros((GROUPS, heads_group, P_SIZE, N), jnp.float32)
    last_state, (core_out, entry_state) = lax.scan(forward_step, initial, (decay_log, signal_f, map_f, read_f))
    with_skip = (core_out + skip_scale * signal_f).reshape(length, GROUPS, group_width)
    gate_f = gate_input.astype(jnp.float32).reshape(length, GROUPS, group_width)
    sigmoid_gate = jax.nn.sigmoid(gate_f)
    silu_gate = gate_f * sigmoid_gate
    gated_out = with_skip * silu_gate
    inv_rms = lax.rsqrt(lax.optimization_barrier(jnp.mean(gated_out * gated_out, axis=-1, keepdims=True)) + 1e-05)
    gain_f = norm_gain.reshape(GROUPS, group_width)
    normed = (gated_out * inv_rms * gain_f).reshape(length, INNER).astype(jnp.bfloat16)
    layer_out = jnp.dot(normed, out_weight, preferred_element_type=jnp.float32).astype(jnp.bfloat16)
    dnormed = jnp.dot(out_grad, out_weight.T, preferred_element_type=jnp.float32).astype(jnp.bfloat16)
    dnormed = lax.optimization_barrier(dnormed).astype(jnp.float32).reshape(length, GROUPS, group_width)
    weight_grad = jnp.dot(normed.T, out_grad, preferred_element_type=jnp.float32)
    gain_grad = lax.optimization_barrier(jnp.sum(dnormed * gated_out * inv_rms, axis=0)).reshape(INNER)
    scaled_grad = gain_f * dnormed
    dgated = inv_rms * scaled_grad - gated_out * inv_rms ** 3 * lax.optimization_barrier(jnp.mean(scaled_grad * gated_out, axis=-1, keepdims=True))
    gate_grad = (dgated * with_skip * sigmoid_gate * (1.0 + gate_f * (1.0 - sigmoid_gate))).reshape(length, INNER)
    grad_y = (dgated * silu_gate).reshape(span_count, SPAN, GROUPS, heads_group, P_SIZE)
    skip_grad = lax.optimization_barrier(jnp.sum(grad_y * signal_f, axis=(0, 1, 4))).reshape(HEADS)
    first_grad, (core_grad, map_grad, read_grad, log_slope) = lax.scan(backward_step, jnp.zeros((GROUPS, heads_group, P_SIZE, N), jnp.float32), (decay_log, signal_f, map_f, read_f, grad_y, core_out, entry_state), reverse=True)
    signal_grad = (core_grad + skip_scale * grad_y).reshape(length, INNER)
    decay_grad = log_slope.transpose(2, 3, 0, 1).reshape(HEADS, length)
    return (layer_out, signal_grad, gate_grad, map_grad.reshape(length, GROUPS * N), read_grad.reshape(length, GROUPS * N), decay_grad, skip_grad, gain_grad, weight_grad)
```

```python
from functools import partial

import jax
import jax.numpy as jnp
from jax import lax
from jax.experimental import pallas as pl
from jax.experimental.pallas import tpu as pltpu
from jax.sharding import PartitionSpec as P

P_SIZE = 64
N = 128
CHUNK = 256
PIECE = 256
LAG = 5
F32 = jnp.float32
BF16 = jnp.bfloat16
VMEM_LIMIT = 58 * 1024 * 1024
MESH = pl.DeviceIdType.MESH

NN = (((1,), (0,)), ((), ()))
NT = (((1,), (1,)), ((), ()))
TN = (((0,), (0,)), ((), ()))


def mm(a, b, dims=NN):
    return lax.dot_general(a, b, dims, preferred_element_type=F32)


def spread(factor, width):
    rows = factor.shape[0]
    left = lax.broadcasted_iota(jnp.int32, (rows, 128), 1) < P_SIZE
    pairs = []
    for k in range(width // 128):
        a = jnp.broadcast_to(factor[:, 2 * k : 2 * k + 1], (rows, 128))
        b = jnp.broadcast_to(factor[:, 2 * k + 1 : 2 * k + 2], (rows, 128))
        pairs.append(jnp.where(left, a, b))
    return jnp.concatenate(pairs, axis=1)


def cumulated(log_row):
    heads, length = log_row.shape
    hi = log_row.astype(BF16).astype(F32)
    rest = log_row - hi
    mid = rest.astype(BF16).astype(F32)
    low = rest - mid
    parts = jnp.concatenate([hi, mid, low, jnp.zeros_like(hi)], axis=0).astype(BF16)
    upper = (
        lax.broadcasted_iota(jnp.int32, (length, length), 0)
        <= lax.broadcasted_iota(jnp.int32, (length, length), 1)
    )
    sums = mm(parts, jnp.where(upper, 1.0, 0.0).astype(BF16))
    row = sums[0:heads] + sums[heads : 2 * heads] + sums[2 * heads : 3 * heads]
    col = jnp.transpose(jnp.concatenate([row] * (128 // heads), axis=0))
    return row, col


def layer_kernel(
    sizes,
    x_hbm, z_hbm, b_hbm, c_hbm, log_hbm, w_hbm, og_hbm, skip_ref, gain_ref,
    layer_hbm, signal_hbm, gate_hbm, map_hbm, read_hbm, decay_hbm, param_hbm, weight_hbm,
    x_v, z_v, b_v, c_v, log_v, w_v, rows_v,
    row_t, col_t, start_t, close_t,
    own_s, own_f, got_s, got_f, turned, arriving,
    core_v, entry_v, normed_v, other_n, trans_n,
    dy_v, gate_v, signal_v, map_v, read_v, decay_v,
    out_flow, own_l, got_l, turned_l, arriving_l, sums_v, got_p, param_v,
    layer_part, layer_got, layer_v,
    stage, from_left, from_right, fin,
    in_sem, out_sem, own_row_sem,
    row_send, row_recv, ex_send, ex_recv, norm_send, norm_recv, lay_send, lay_recv,
    line_send, left_recv, right_recv, fin_left, fin_right, fin_recv, side_send, side_recv, fin_out,
):
    n, nh, tokens, groups, width, model = sizes
    spans = tokens // CHUNK
    half_w = width // 2
    heads = width // P_SIZE
    block = og_hbm.shape[0]
    share = 16
    holders = N // share
    stride = max(1, n // holders)
    line = n // 2
    root = (line - 1) // 2
    cols = model // PIECE
    halves = model // 2

    me = lax.axis_index("ctx")
    hd = lax.axis_index("head")
    side = lax.rem(me, 2)
    other = 1 - side
    pair = me + 1 - 2 * side
    at_line = me // 2
    core = lax.rem(hd, 2)
    sibling = hd + 1 - 2 * core

    def wrap(i, size):
        return lax.rem(i + size, size)

    def when(cond, fn):
        if cond is True:
            fn()
        else:
            pl.when(cond)(fn)

    inputs = [
        (log_hbm, log_v), (b_hbm, b_v), (x_hbm, x_v), (c_hbm, c_v), (z_hbm, z_v), (w_hbm, w_v),
    ]
    loads = [pltpu.make_async_copy(a, b, in_sem.at[i]) for i, (a, b) in enumerate(inputs)]
    for load in loads:
        load.start()

    def row_at(which, head, q):
        at = pl.ds(pl.multiple_of(head * block, 16), block)
        return rows_v.at[which, at, pl.ds(q * halves, halves)]

    own_rows = [
        pltpu.make_async_copy(
            og_hbm.at[:, pl.ds(q * halves, halves)], row_at(side, hd, q), own_row_sem.at[q]
        )
        for q in range(2)
    ]
    for copy in own_rows:
        copy.start()

    barrier = pltpu.get_barrier_semaphore()
    for k in range(1, n):
        pl.semaphore_signal(
            barrier, inc=1, device_id={"ctx": wrap(me + k, n)}, device_id_type=MESH
        )
    for k in range(1, nh):
        pl.semaphore_signal(
            barrier, inc=1, device_id={"head": wrap(hd + k, nh)}, device_id_type=MESH
        )
    pl.semaphore_wait(barrier, n - 1 + nh - 1)

    chips = nh // 2

    def row_copy(q, kind, k):
        x_next = wrap(hd + 2 * k, nh)
        x_from = wrap(hd - 2 * k, nh)
        if kind in ("x", "sib", "side"):
            src = og_hbm.at[:, pl.ds(q * halves, halves)]
            dst = row_at(side, hd, q)
        elif kind == "x_sib":
            src = dst = row_at(side, x_from, q)
        elif kind in ("side_sib", "side_x"):
            src = dst = row_at(other, hd, q)
        else:
            src = dst = row_at(other, x_from, q)
        if kind in ("x", "side_x"):
            target = {"head": x_next}
        elif kind == "side":
            target = {"ctx": pair}
        else:
            target = {"head": sibling}
        i = {"sib": 0, "side": 1, "side_sib": 2}.get(kind)
        if i is None:
            i = 3 + {"x": 0, "x_sib": 1, "side_x": 2, "side_x_sib": 3}[kind] * (chips - 1) + k - 1
        return pltpu.make_async_remote_copy(
            src, dst, row_send.at[q, i], row_recv.at[q, i], device_id=target, device_id_type=MESH
        )

    away = range(1, chips)
    row_all = [("sib", 0), ("side", 0), ("side_sib", 0)]
    row_all += [(kind, k) for kind in ("x", "x_sib", "side_x", "side_x_sib") for k in away]
    for q in range(2):
        for k in away:
            row_copy(q, "x", k).start()
        row_copy(q, "side", 0).start()
        row_copy(q, "sib", 0).start()

    def rows_relay(q):
        row_copy(q, "side", 0).wait_recv()
        for k in away:
            row_copy(q, "side_x", k).start()
        row_copy(q, "side_sib", 0).start()
        for k in away:
            row_copy(q, "x", k).wait_recv()
            row_copy(q, "x_sib", k).start()

    def rows_end(q):
        for k in away:
            row_copy(q, "side_x", k).wait_recv()
            row_copy(q, "side_x_sib", k).start()
        row_copy(q, "sib", 0).wait_recv()
        own_rows[q].wait()
        for k in away:
            row_copy(q, "x_sib", k).wait_recv()

    def rows_last(q):
        row_copy(q, "side_sib", 0).wait_recv()
        for k in away:
            row_copy(q, "side_x_sib", k).wait_recv()

    is_holder = True if stride == 1 else lax.rem(me, stride) == 0
    my_share = pl.multiple_of(me // stride * share, share)

    def holds(i):
        return True if stride == 1 else lax.rem(i, stride) == 0

    def exchange(base, state, fade, got, got_fade, result, into):
        def first(k):
            to = wrap(me + k, n)
            part = pl.ds(pl.multiple_of(to // stride * share, share), share)
            return pltpu.make_async_remote_copy(
                state.at[:, part, :], got.at[me],
                ex_send.at[base, k], ex_recv.at[base, k],
                device_id={"ctx": to}, device_id_type=MESH,
            )

        def beside(k):
            return pltpu.make_async_remote_copy(
                fade, got_fade.at[me],
                ex_send.at[base + 1, k], ex_recv.at[base + 1, k],
                device_id={"ctx": wrap(me + k, n)}, device_id_type=MESH,
            )

        def second(k):
            to = wrap(me + k, n)
            return pltpu.make_async_remote_copy(
                result.at[to], into.at[:, pl.ds(my_share, share), :],
                ex_send.at[base + 2, k], ex_recv.at[base + 2, k],
                device_id={"ctx": to}, device_id_type=MESH,
            )

        return first, beside, second

    def send_shares(copies, state, got, to_all, fade, got_fade):
        first, beside, _ = copies
        for k in range(1, n):
            def _(k=k):
                first(k).start()
                if not to_all:
                    beside(k).start()
            when(holds(wrap(me + k, n)), _)
            if to_all:
                beside(k).start()

        def _():
            got[pl.ds(me, 1)] = state[:, pl.ds(my_share, share), :][None]
        when(is_holder, _)
        got_fade[pl.ds(me, 1)] = fade[...][None]

    def carry_shares(copies, got, fades, result, into, reverse):
        first, beside, second = copies

        def _():
            for k in range(1, n):
                first(k).wait_recv()
                if not reverse:
                    beside(k).wait_recv()
            carried = jnp.zeros((groups, share, width), F32)
            for d in reversed(range(n)) if reverse else range(n):
                result[d] = carried.astype(BF16)
                carried = fades[d][:, None, :] * carried + got[d].astype(F32)
            for k in range(1, n):
                second(k).start()
            into[:, pl.ds(my_share, share), :] = result[me]
        when(is_holder, _)

    def take_shares(copies):
        for k in range(1, n):
            def _(k=k):
                copies[2](k).wait_recv()
            when(holds(wrap(me - k, n)), _)

    def drain_shares(copies, to_all):
        first, beside, second = copies
        for k in range(1, n):
            def _(k=k):
                first(k).wait_send()
                if not to_all:
                    beside(k).wait_send()
            when(holds(wrap(me + k, n)), _)
            if to_all:
                beside(k).wait_send()
            def _(k=k):
                second(k).wait_send()
            when(is_holder, _)

    def at(c):
        return slice(c * CHUNK, (c + 1) * CHUNK)

    def wide(g):
        return slice(g * width, (g + 1) * width)

    def narrow(g):
        return slice(g * N, (g + 1) * N)

    left = lax.broadcasted_iota(jnp.int32, (CHUNK, 128), 1) < P_SIZE

    def local_state(g):
        state = jnp.zeros((N, width), F32)
        decay = jnp.ones((1, width), F32)
        for c in range(spans):
            row, col = cumulated(log_v[g * heads : (g + 1) * heads, at(c)])
            i = g * spans + c
            row_t[i] = row
            col_t[i] = col
            col = col[:, :heads]
            from_start = spread(jnp.exp(col), width)
            to_closing = spread(jnp.exp(col[-1:, :] - col), width)
            start_t[i] = from_start
            close_t[i] = to_closing
            span = from_start[-1:, :]
            scaled = (x_v[at(c), wide(g)].astype(F32) * to_closing).astype(BF16)
            state = state * span + mm(b_v[at(c), narrow(g)], scaled, TN)
            decay = decay * span
        own_s[g] = state.astype(BF16)
        own_f[g : g + 1, :] = decay

    def intra(g, c):
        i = g * spans + c
        row, col = row_t[i], col_t[i]
        lower = (
            lax.broadcasted_iota(jnp.int32, (CHUNK, CHUNK), 0)
            >= lax.broadcasted_iota(jnp.int32, (CHUNK, CHUNK), 1)
        )
        x = x_v[at(c), wide(g)]
        inner = mm(c_v[at(c), narrow(g)], b_v[at(c), narrow(g)], NT)
        for k in range(width // 128):
            two = x[:, 128 * k : 128 * k + 128]
            parts = []
            for h in (2 * k, 2 * k + 1):
                gap = jnp.where(lower, col[:, h : h + 1] - row[h : h + 1, :], -1e30)
                parts.append(mm((jnp.exp(gap) * inner).astype(BF16), two))
            lanes = slice(g * width + 128 * k, g * width + 128 * k + 128)
            core_v[at(c), lanes] = jnp.where(left, parts[0], parts[1])

    def norm_copy(g):
        return pltpu.make_async_remote_copy(
            normed_v.at[g, other], other_n.at[g], norm_send.at[g], norm_recv.at[g],
            device_id={"ctx": pair}, device_id_type=MESH,
        )

    def forward(g):
        state = arriving[g].astype(F32)
        for c in range(spans):
            i = g * spans + c
            entry = state.astype(BF16)
            entry_v[i] = entry
            xf = x_v[at(c), wide(g)].astype(F32)
            from_start = start_t[i]
            core_now = core_v[at(c), wide(g)] + from_start * mm(c_v[at(c), narrow(g)], entry)
            core_v[at(c), wide(g)] = core_now
            y = core_now + skip_ref[:, wide(g)] * xf
            z = z_v[at(c), wide(g)].astype(F32)
            gated = y * (z * jax.nn.sigmoid(z))
            inv = lax.rsqrt(jnp.mean(gated * gated, axis=1, keepdims=True) + 1e-05)
            normed = (gated * inv * gain_ref[:, wide(g)]).astype(BF16)
            normed_v[g, 0, at(c), :] = normed[:, :half_w]
            normed_v[g, 1, at(c), :] = normed[:, half_w:]
            if c < spans - 1:
                scaled = (xf * close_t[i]).astype(BF16)
                state = state * from_start[-1:, :] + mm(b_v[at(c), narrow(g)], scaled, TN)
        norm_copy(g).start()
        trans_n[g, :, pl.ds(pl.multiple_of(side * tokens, CHUNK), tokens)] = jnp.transpose(
            normed_v[g, side]
        )

    def out_copy(i, g, c):
        src, dst = ((gate_v, gate_hbm), (signal_v, signal_hbm))[i]
        return pltpu.make_async_copy(
            src.at[at(c), wide(g)], dst.at[at(c), wide(g)], out_sem.at[i, g * spans + c]
        )

    def middle(g, c):
        i = g * spans + c
        from_start = start_t[i]
        gain = gain_ref[:, wide(g)]
        dn = mm(rows_v[side, at(c), :], w_v[wide(g), :], NT).astype(BF16).astype(F32)
        xf = x_v[at(c), wide(g)].astype(F32)
        z = z_v[at(c), wide(g)].astype(F32)
        y = core_v[at(c), wide(g)] + skip_ref[:, wide(g)] * xf
        s = jax.nn.sigmoid(z)
        silu = z * s
        gated = y * silu
        inv = lax.rsqrt(jnp.mean(gated * gated, axis=1, keepdims=True) + 1e-05)
        gain_sum = jnp.sum(dn * gated * inv, axis=0, keepdims=True)
        scaled = gain * dn
        mean = jnp.mean(scaled * gated, axis=1, keepdims=True)
        dgated = inv * scaled - gated * (inv * inv * inv * mean)
        gate_v[at(c), wide(g)] = dgated * y * s * (1.0 + z * (1.0 - s))
        out_copy(0, g, c).start()
        dy = dgated * silu
        dy_v[at(c), wide(g)] = dy
        skip_sum = jnp.sum(dy * xf, axis=0, keepdims=True)
        flow = mm(c_v[at(c), narrow(g)], (dy * from_start).astype(BF16), TN)
        if c == spans - 1:
            sums_v[g : g + 1, :] = gain_sum
            sums_v[groups + g : groups + g + 1, :] = skip_sum
            out_flow[g] = flow
        else:
            sums_v[g : g + 1, :] += gain_sum
            sums_v[groups + g : groups + g + 1, :] += skip_sum
            out_flow[g] = out_flow[g] * from_start[-1:, :] + flow
        if c == 0:
            own_l[g] = out_flow[g].astype(BF16)

    def layer_terms(j):
        cut = slice(j * 512, (j + 1) * 512)
        total = jnp.zeros((tokens, 512), F32)
        for g in range(groups):
            both = jnp.concatenate([normed_v[g, 0], normed_v[g, 1]], axis=1)
            total += mm(both, w_v[wide(g), cut])
        layer_part[:, cut] = total.astype(BF16)

    def layer_copy(k):
        to = wrap(hd + k, nh)
        return pltpu.make_async_remote_copy(
            layer_part.at[pl.ds(pl.multiple_of(to * block, 16), block), :], layer_got.at[k - 1],
            lay_send.at[k - 1], lay_recv.at[k - 1], device_id={"head": to}, device_id_type=MESH,
        )

    def layer_sum():
        total = layer_part[pl.ds(pl.multiple_of(hd * block, 16), block), :].astype(F32)
        for k in range(1, nh):
            layer_copy(k).wait_recv()
            total += layer_got[k - 1].astype(F32)
        layer_v[...] = total.astype(BF16)

    def back_inner(g, c):
        i = g * spans + c
        row, col = row_t[i], col_t[i]
        upper = (
            lax.broadcasted_iota(jnp.int32, (CHUNK, CHUNK), 0)
            <= lax.broadcasted_iota(jnp.int32, (CHUNK, CHUNK), 1)
        )
        x = x_v[at(c), wide(g)]
        xf = x.astype(F32)
        dyf = dy_v[at(c), wide(g)]
        dy = dyf.astype(BF16)
        bm, cm = b_v[at(c), narrow(g)], c_v[at(c), narrow(g)]
        inner = mm(bm, cm, NT)
        pair_sum = jnp.zeros((CHUNK, CHUNK), F32)
        for k in range(width // 128):
            cut = slice(128 * k, 128 * k + 128)
            x_two, dy_two = xf[:, cut], dy[:, cut]
            parts = []
            for h, lanes in ((2 * k, left), (2 * k + 1, ~left)):
                gap = jnp.where(upper, row[h : h + 1, :] - col[:, h : h + 1], -1e30)
                fade = jnp.exp(gap)
                parts.append(mm((fade * inner).astype(BF16), dy_two))
                one = jnp.where(lanes, x_two, 0.0).astype(BF16)
                pair_sum += mm(one, dy_two, NT) * fade
            lanes = slice(g * width + 128 * k, g * width + 128 * k + 128)
            signal_v[at(c), lanes] = jnp.where(left, parts[0], parts[1])
        pair_sum = pair_sum.astype(BF16)
        map_v[at(c), narrow(g)] = mm(pair_sum, cm)
        dy_start = (dyf * start_t[i]).astype(BF16)
        read_v[at(c), narrow(g)] = mm(pair_sum, bm, TN) + mm(dy_start, entry_v[i], NT)

    def back_outer(g):
        own = (
            lax.broadcasted_iota(jnp.int32, (heads, width), 1) // P_SIZE
            == lax.broadcasted_iota(jnp.int32, (heads, width), 0)
        )
        own = jnp.where(own, 1.0, 0.0).astype(BF16)
        flow = arriving_l[g].astype(F32)
        for c in reversed(range(spans)):
            i = g * spans + c
            out = flow.astype(BF16)
            xf = x_v[at(c), wide(g)].astype(F32)
            dyf = dy_v[at(c), wide(g)]
            to_closing = close_t[i]
            core_grad = signal_v[at(c), wide(g)] + to_closing * mm(b_v[at(c), narrow(g)], out)
            signal_v[at(c), wide(g)] = core_grad + skip_ref[:, wide(g)] * dyf
            out_copy(1, g, c).start()
            map_v[at(c), narrow(g)] += mm((xf * to_closing).astype(BF16), out, NT)
            slope = dyf * core_v[at(c), wide(g)] - xf * core_grad
            hi = slope.astype(BF16)
            low = (slope - hi.astype(F32)).astype(BF16)
            decay_v[g * heads : (g + 1) * heads, at(c)] = mm(own, hi, NT) + mm(own, low, NT)
            if c > 0:
                from_start = start_t[i]
                dy_start = (dyf * from_start).astype(BF16)
                flow = flow * from_start[-1:, :] + mm(c_v[at(c), narrow(g)], dy_start, TN)

    pieces = [(g, j) for g in range(groups) for j in range(cols)]
    below, above, here = at_line < root, at_line > root, at_line == root
    first_end, last_end = at_line == 0, at_line == line - 1
    lower_id, upper_id = wrap(me - 2, n), wrap(me + 2, n)

    def remote(src, dst, send, recv, to):
        return pltpu.make_async_remote_copy(
            src, dst, send, recv, device_id={"ctx": to}, device_id_type=MESH
        )

    def term_up(i):
        return remote(stage.at[i], from_left.at[i], line_send.at[i], left_recv.at[i], upper_id)

    def term_down(i):
        return remote(stage.at[i], from_right.at[i], line_send.at[i], right_recv.at[i], lower_id)

    def fin_at(i, which):
        g, j = pieces[i]
        return fin.at[g, which, j]

    def fin_down(i):
        return remote(fin_at(i, side), fin_at(i, side), fin_left.at[i], fin_recv.at[i], lower_id)

    def fin_up(i):
        return remote(fin_at(i, side), fin_at(i, side), fin_right.at[i], fin_recv.at[i], upper_id)

    def fin_side(i):
        return remote(fin_at(i, side), fin_at(i, side), side_send.at[i], side_recv.at[i], pair)

    def fin_side_in(i):
        return remote(fin_at(i, other), fin_at(i, other), side_send.at[i], side_recv.at[i], pair)

    def fin_store(i, which, slot):
        g, j = pieces[i]
        return pltpu.make_async_copy(
            fin_at(i, which), weight_hbm.at[g, which, j], fin_out.at[slot, i]
        )

    def reduce_piece(i):
        g, j = pieces[i]
        if j == 0:
            norm_copy(g).wait_recv()
            trans_n[g, :, pl.ds(pl.multiple_of(other * tokens, CHUNK), tokens)] = jnp.transpose(
                other_n[g]
            )
        cut = slice(j * PIECE, (j + 1) * PIECE)
        own = mm(trans_n[g, :, :tokens], rows_v[0, :, cut])
        own += mm(trans_n[g, :, tokens:], rows_v[1, :, cut])

        @pl.when(below)
        def _():
            @pl.when(first_end)
            def _():
                stage[i] = own.astype(BF16)

            @pl.when(jnp.logical_not(first_end))
            def _():
                term_up(i).wait_recv()
                stage[i] = (own + from_left[i].astype(F32)).astype(BF16)

            term_up(i).start()

        @pl.when(above)
        def _():
            @pl.when(last_end)
            def _():
                stage[i] = own.astype(BF16)

            @pl.when(jnp.logical_not(last_end))
            def _():
                term_down(i).wait_recv()
                stage[i] = (own + from_right[i].astype(F32)).astype(BF16)

            term_down(i).start()

        @pl.when(here)
        def _():
            total = own
            if root > 0:
                term_up(i).wait_recv()
                total += from_left[i].astype(F32)
            if root < line - 1:
                term_down(i).wait_recv()
                total += from_right[i].astype(F32)
            fin[g, pl.ds(side, 1), j] = total.astype(BF16)[None]
            if root > 0:
                fin_down(i).start()
            if root < line - 1:
                fin_up(i).start()
            fin_side(i).start()
            fin_store(i, side, 0).start()

    def pass_on(i):
        @pl.when(jnp.logical_not(here))
        def _():
            fin_up(i).wait_recv()

            @pl.when(jnp.logical_and(below, jnp.logical_not(first_end)))
            def _():
                fin_down(i).start()

            @pl.when(jnp.logical_and(above, jnp.logical_not(last_end)))
            def _():
                fin_up(i).start()

            fin_side(i).start()
            fin_store(i, side, 0).start()

    def take_side(i):
        fin_side_in(i).wait_recv()
        fin_store(i, other, 1).start()

    def drain_piece(i):
        @pl.when(jnp.logical_not(here))
        def _():
            term_up(i).wait_send()

        goes_down = jnp.logical_or(
            jnp.logical_and(here, jnp.logical_not(first_end)),
            jnp.logical_and(below, jnp.logical_not(first_end)),
        )
        goes_up = jnp.logical_or(
            jnp.logical_and(here, jnp.logical_not(last_end)),
            jnp.logical_and(above, jnp.logical_not(last_end)),
        )

        @pl.when(goes_down)
        def _():
            fin_down(i).wait_send()

        @pl.when(goes_up)
        def _():
            fin_up(i).wait_send()

        fin_side(i).wait_send()
        fin_store(i, side, 0).wait()
        fin_store(i, other, 1).wait()

    ex_f = exchange(0, own_s, own_f, got_s, got_f, turned, arriving)
    ex_b = exchange(3, own_l, sums_v, got_l, got_p, turned_l, arriving_l)

    for i in (0, 1, 2):
        loads[i].wait()
    for g in range(groups):
        local_state(g)
    send_shares(ex_f, own_s, got_s, False, own_f, got_f)
    loads[3].wait()
    for c in range(spans):
        intra(0, c)
    carry_shares(ex_f, got_s, got_f, turned, arriving, False)
    rows_relay(0)
    for g in range(1, groups):
        for c in range(spans):
            intra(g, c)
    loads[4].wait()
    take_shares(ex_f)
    for g in range(groups):
        forward(g)
    rows_relay(1)
    rows_end(0)
    rows_last(0)
    loads[5].wait()

    def rows_full():
        rows_end(1)
        rows_last(1)

    def start_layer():
        for k in range(1, nh):
            layer_copy(k).start()

    def later_send():
        send_shares(ex_b, own_l, got_l, True, sums_v, got_p)

    def later_carry():
        carry_shares(ex_b, got_l, got_f, turned_l, arriving_l, True)

    def narrow_out():
        for i, (src, dst) in enumerate(((map_v, map_hbm), (read_v, read_hbm), (decay_v, decay_hbm))):
            pltpu.make_async_copy(src, dst, out_sem.at[2 + i, 0]).start()

    def params_sum():
        for k in range(1, n):
            ex_b[1](k).wait_recv()
        total = jnp.zeros((2 * groups, width), F32)
        for d in range(n):
            total += got_p[d]
        param_v[...] = total

    items = [partial(layer_terms, j) for j in range(model // 512)]
    items += [start_layer]
    items += [partial(middle, g, c) for g in range(groups) for c in reversed(range(spans))]
    items += [later_send]
    inner_items = [partial(back_inner, g, c) for g in range(groups) for c in range(spans)]
    items += inner_items[: len(inner_items) // 2]
    items += [later_carry]
    items += inner_items[len(inner_items) // 2 :]
    items += [lambda: take_shares(ex_b)]
    items += [partial(back_outer, g) for g in range(groups)]
    items += [narrow_out, params_sum, layer_sum]

    count = len(pieces)
    ticks = count + LAG + 1
    done = 0
    for t in range(ticks):
        if t == cols // 2 - 1:
            rows_full()
        if t < count:
            reduce_piece(t)
        if 0 <= t - LAG < count:
            pass_on(t - LAG)
        if 0 <= t - LAG - 1 < count:
            take_side(t - LAG - 1)
        want = min(len(items) * (t + 1) // count, len(items))
        while done < want:
            items[done]()
            done += 1
    while done < len(items):
        items[done]()
        done += 1

    pltpu.make_async_copy(layer_v, layer_hbm, out_sem.at[5, 0]).start()
    pltpu.make_async_copy(param_v, param_hbm, out_sem.at[6, 0]).start()

    for q in range(2):
        for kind, k in row_all:
            row_copy(q, kind, k).wait_send()
    drain_shares(ex_f, False)
    drain_shares(ex_b, True)
    for g in range(groups):
        norm_copy(g).wait_send()
    for k in range(1, nh):
        layer_copy(k).wait_send()
    for i in range(count):
        drain_piece(i)
    for i in range(2):
        for g in range(groups):
            for c in range(spans):
                out_copy(i, g, c).wait()
    for i, (src, dst) in enumerate(
        ((map_v, map_hbm), (read_v, read_hbm), (decay_v, decay_hbm), (layer_v, layer_hbm), (param_v, param_hbm))
    ):
        pltpu.make_async_copy(src, dst, out_sem.at[2 + i, 0]).wait()


def widen_kernel(in_ref, out_ref):
    for j in range(in_ref.shape[2]):
        out_ref[:, j * PIECE : (j + 1) * PIECE] = in_ref[0, 0, j].astype(F32)


def on_device(
    n, nh,
    signal, gate_input, input_map, readout, log_decay, skip_gain, norm_gain, out_weight, out_grad,
):
    tokens, features = signal.shape
    heads = log_decay.shape[0]
    groups = input_map.shape[1] // N
    width = features // groups
    model = out_weight.shape[1]
    block = out_grad.shape[0]
    spans = tokens // CHUNK
    cols = model // PIECE
    count = groups * cols
    half_w = width // 2
    chips = nh // 2
    sds = jax.ShapeDtypeStruct
    vm = pltpu.VMEM
    dma = pltpu.SemaphoreType.DMA

    skip = jnp.repeat(skip_gain, P_SIZE).reshape(1, features)
    gain = norm_gain.reshape(1, features)
    hbm = pl.BlockSpec(memory_space=pl.ANY)
    sizes = (n, nh, tokens, groups, width, model)
    kinds = 3 + 4 * (chips - 1)
    all_spans = groups * spans
    layer_out, signal_grad, gate_grad, map_grad, read_grad, decay_grad, sums, weight = pl.pallas_call(
        partial(layer_kernel, sizes),
        in_specs=[hbm] * 7 + [pl.BlockSpec(memory_space=pltpu.VMEM)] * 2,
        out_specs=[hbm] * 8,
        out_shape=[
            sds((block, model), BF16),
            sds((tokens, features), F32),
            sds((tokens, features), F32),
            sds((tokens, groups * N), F32),
            sds((tokens, groups * N), F32),
            sds((heads, tokens), F32),
            sds((2 * groups, width), F32),
            sds((groups, 2, cols, half_w, PIECE), BF16),
        ],
        scratch_shapes=[
            vm((tokens, features), BF16), vm((tokens, features), BF16),
            vm((tokens, groups * N), BF16), vm((tokens, groups * N), BF16),
            vm((heads, tokens), F32), vm((features, model), BF16), vm((2, tokens, model), BF16),
            vm((all_spans, heads // groups, CHUNK), F32), vm((all_spans, CHUNK, 128), F32),
            vm((all_spans, CHUNK, width), F32), vm((all_spans, CHUNK, width), F32),
            vm((groups, N, width), BF16), vm((groups, width), F32),
            vm((n, groups, 16, width), BF16), vm((n, groups, width), F32),
            vm((n, groups, 16, width), BF16), vm((groups, N, width), BF16),
            vm((tokens, features), F32), vm((all_spans, N, width), BF16),
            vm((groups, 2, tokens, half_w), BF16), vm((groups, tokens, half_w), BF16),
            vm((groups, half_w, 2 * tokens), BF16),
            vm((tokens, features), F32), vm((tokens, features), F32), vm((tokens, features), F32),
            vm((tokens, groups * N), F32), vm((tokens, groups * N), F32), vm((heads, tokens), F32),
            vm((groups, N, width), F32), vm((groups, N, width), BF16),
            vm((n, groups, 16, width), BF16), vm((n, groups, 16, width), BF16),
            vm((groups, N, width), BF16),
            vm((2 * groups, width), F32), vm((n, 2 * groups, width), F32), vm((2 * groups, width), F32),
            vm((tokens, model), BF16), vm((nh - 1, block, model), BF16), vm((block, model), BF16),
            vm((count, half_w, PIECE), BF16), vm((count, half_w, PIECE), BF16),
            vm((count, half_w, PIECE), BF16), vm((groups, 2, cols, half_w, PIECE), BF16),
            dma((6,)), dma((7, all_spans)), dma((2,)),
            dma((2, kinds)), dma((2, kinds)), dma((6, n)), dma((6, n)),
            dma((groups,)), dma((groups,)), dma((nh - 1,)), dma((nh - 1,)),
            dma((count,)), dma((count,)), dma((count,)), dma((count,)), dma((count,)), dma((count,)),
            dma((count,)), dma((count,)), dma((2, count)),
        ],
        compiler_params=pltpu.CompilerParams(
            collective_id=0, has_side_effects=True, vmem_limit_bytes=VMEM_LIMIT
        ),
        name="layer",
    )(signal, gate_input, input_map, readout, log_decay, out_weight, out_grad, skip, gain)

    weight_grad = pl.pallas_call(
        widen_kernel,
        grid=(groups, 2),
        in_specs=[pl.BlockSpec((1, 1, cols, half_w, PIECE), lambda g, s: (g, s, 0, 0, 0))],
        out_specs=pl.BlockSpec((half_w, model), lambda g, s: (2 * g + s, 0)),
        out_shape=sds((features, model), F32),
        name="widen",
    )(weight)

    gain_grad = sums[:groups].reshape(features)
    skip_grad = jnp.sum(sums[groups:].reshape(heads, P_SIZE), axis=1)
    return (
        layer_out, signal_grad, gate_grad, map_grad, read_grad, decay_grad,
        skip_grad, gain_grad, weight_grad,
    )


def solution(mesh):
    return jax.shard_map(
        partial(on_device, mesh.shape["ctx"], mesh.shape["head"]),
        mesh=mesh,
        in_specs=(
            P("ctx", "head"),
            P("ctx", "head"),
            P("ctx", "head"),
            P("ctx", "head"),
            P("head", "ctx"),
            P("head"),
            P("head"),
            P("head", None),
            P(("ctx", "head"), None),
        ),
        out_specs=(
            P(("ctx", "head"), None),
            P("ctx", "head"),
            P("ctx", "head"),
            P("ctx", "head"),
            P("ctx", "head"),
            P("head", "ctx"),
            P("head"),
            P("head"),
            P("head", None),
        ),
        check_vma=False,
    )
```

```python
from functools import partial

import jax
import jax.numpy as jnp
from jax import lax
from jax.experimental import pallas as pl
from jax.experimental.pallas import tpu as pltpu
from jax.sharding import PartitionSpec as P

P_SIZE = 64
N = 128
CHUNK = 256
PIECE = 256
LAG = 4
LAG_HOP = 3
LAG_SIDE = 3
F32 = jnp.float32
BF16 = jnp.bfloat16
VMEM_LIMIT = 46 * 1024 * 1024
MESH = pl.DeviceIdType.MESH

NN = (((1,), (0,)), ((), ()))
NT = (((1,), (1,)), ((), ()))
TN = (((0,), (0,)), ((), ()))


def mm(a, b, dims=NN):
    return lax.dot_general(a, b, dims, preferred_element_type=F32)


def spread(factor, width):
    rows = factor.shape[0]
    left = lax.broadcasted_iota(jnp.int32, (rows, 128), 1) < P_SIZE
    pairs = []
    for k in range(width // 128):
        a = jnp.broadcast_to(factor[:, 2 * k : 2 * k + 1], (rows, 128))
        b = jnp.broadcast_to(factor[:, 2 * k + 1 : 2 * k + 2], (rows, 128))
        pairs.append(jnp.where(left, a, b))
    return jnp.concatenate(pairs, axis=1)


def cumulated(log_row):
    heads, length = log_row.shape
    hi = log_row.astype(BF16).astype(F32)
    rest = log_row - hi
    mid = rest.astype(BF16).astype(F32)
    low = rest - mid
    parts = jnp.concatenate([hi, mid, low, jnp.zeros_like(hi)], axis=0).astype(BF16)
    upper = (
        lax.broadcasted_iota(jnp.int32, (length, length), 0)
        <= lax.broadcasted_iota(jnp.int32, (length, length), 1)
    )
    sums = mm(parts, jnp.where(upper, 1.0, 0.0).astype(BF16))
    row = sums[0:heads] + sums[heads : 2 * heads] + sums[2 * heads : 3 * heads]
    col = jnp.transpose(jnp.concatenate([row] * (128 // heads), axis=0))
    return row, col


def layer_kernel(
    sizes,
    x_hbm, z_hbm, b_hbm, c_hbm, log_hbm, w_hbm, og_hbm, skip_s, gain_ref,
    layer_v, signal_v, gate_v, map_v, read_v, decay_v, gain_out, skip_out, fin,
    x_v, z_v, b_v, c_v, log_v, w_v, rows_v,
    row_t, col_t, start_t, close_t,
    own_s, own_f, got_s, got_f, turned, arriving,
    core_v, entry_v, normed_v, other_n, trans_n,
    dy_v, skip_ref,
    out_flow, own_l, got_l, turned_l, arriving_l, sums_v, got_p,
    layer_part, layer_got,
    stage, from_left, from_right,
    in_sem, own_row_sem,
    row_send, row_recv, ex_send, ex_recv, be_send, be_recv, norm_send, norm_recv, lay_send, lay_recv,
    line_send, left_recv, right_recv, fin_left, fin_right, fin_recv, side_send, side_recv,
):
    n, nh, tokens, groups, width, model = sizes
    spans = tokens // CHUNK
    half_w = width // 2
    heads = width // P_SIZE
    block = og_hbm.shape[0]
    share = 16
    holders = N // share
    stride = max(1, n // holders)
    line = n // 2
    root = (line - 1) // 2
    cols = model // PIECE
    halves = model // 2

    me = lax.axis_index("ctx")
    hd = lax.axis_index("head")
    side = lax.rem(me, 2)
    other = 1 - side
    pair = me + 1 - 2 * side
    at_line = me // 2
    core = lax.rem(hd, 2)
    sibling = hd + 1 - 2 * core

    def wrap(i, size):
        return lax.rem(i + size, size)

    def when(cond, fn):
        if cond is True:
            fn()
        else:
            pl.when(cond)(fn)

    inputs = [
        (log_hbm, log_v), (b_hbm, b_v), (x_hbm, x_v), (c_hbm, c_v), (z_hbm, z_v), (w_hbm, w_v),
    ]
    loads = [pltpu.make_async_copy(a, b, in_sem.at[i]) for i, (a, b) in enumerate(inputs)]
    for load in loads[:3]:
        load.start()

    def row_at(which, head, q):
        at = pl.ds(pl.multiple_of(head * block, 16), block)
        return rows_v.at[which, at, pl.ds(q * halves, halves)]

    own_rows = [
        pltpu.make_async_copy(
            og_hbm.at[:, pl.ds(q * halves, halves)], row_at(side, hd, q), own_row_sem.at[q]
        )
        for q in range(2)
    ]
    for copy in own_rows:
        copy.start()

    barrier = pltpu.get_barrier_semaphore()
    for k in range(1, n):
        pl.semaphore_signal(
            barrier, inc=1, device_id={"ctx": wrap(me + k, n)}, device_id_type=MESH
        )
    for k in range(1, nh):
        pl.semaphore_signal(
            barrier, inc=1, device_id={"head": wrap(hd + k, nh)}, device_id_type=MESH
        )
    pl.semaphore_wait(barrier, n - 1 + nh - 1)

    chips = nh // 2

    def row_copy(q, kind, k):
        x_next = wrap(hd + 2 * k, nh)
        x_from = wrap(hd - 2 * k, nh)
        if kind in ("x", "sib", "side"):
            src = og_hbm.at[:, pl.ds(q * halves, halves)]
            dst = row_at(side, hd, q)
        elif kind == "x_sib":
            src = dst = row_at(side, x_from, q)
        elif kind in ("side_sib", "side_x"):
            src = dst = row_at(other, hd, q)
        else:
            src = dst = row_at(other, x_from, q)
        if kind in ("x", "side_x"):
            target = {"head": x_next}
        elif kind == "side":
            target = {"ctx": pair}
        else:
            target = {"head": sibling}
        i = {"sib": 0, "side": 1, "side_sib": 2}.get(kind)
        if i is None:
            i = 3 + {"x": 0, "x_sib": 1, "side_x": 2, "side_x_sib": 3}[kind] * (chips - 1) + k - 1
        return pltpu.make_async_remote_copy(
            src, dst, row_send.at[q, i], row_recv.at[q, i], device_id=target, device_id_type=MESH
        )

    away = range(1, chips)
    row_all = [("sib", 0), ("side", 0), ("side_sib", 0)]
    row_all += [(kind, k) for kind in ("x", "x_sib", "side_x", "side_x_sib") for k in away]
    for q in range(2):
        for k in away:
            row_copy(q, "x", k).start()
        row_copy(q, "sib", 0).start()

    def rows_side(q):
        row_copy(q, "side", 0).start()

    def rows_relay(q):
        row_copy(q, "side", 0).wait_recv()
        for k in away:
            row_copy(q, "side_x", k).start()
        row_copy(q, "side_sib", 0).start()

    def rows_near(q):
        for k in away:
            row_copy(q, "x", k).wait_recv()
            row_copy(q, "x_sib", k).start()

    def rows_end(q):
        for k in away:
            row_copy(q, "side_x", k).wait_recv()
            row_copy(q, "side_x_sib", k).start()
        row_copy(q, "sib", 0).wait_recv()
        own_rows[q].wait()
        for k in away:
            row_copy(q, "x_sib", k).wait_recv()

    def rows_last(q):
        row_copy(q, "side_sib", 0).wait_recv()
        for k in away:
            row_copy(q, "side_x_sib", k).wait_recv()

    is_holder = True if stride == 1 else lax.rem(me, stride) == 0
    my_share = pl.multiple_of(me // stride * share, share)

    def holds(i):
        return True if stride == 1 else lax.rem(i, stride) == 0

    def exchange(base, g, state, got, result, into):
        def first(k):
            to = wrap(me + k, n)
            part = pl.ds(pl.multiple_of(to // stride * share, share), share)
            return pltpu.make_async_remote_copy(
                state.at[g, part, :], got.at[me, g],
                ex_send.at[base + 2 * g, k], ex_recv.at[base + 2 * g, k],
                device_id={"ctx": to}, device_id_type=MESH,
            )

        def second(k):
            to = wrap(me + k, n)
            return pltpu.make_async_remote_copy(
                result.at[to, g], into.at[g, pl.ds(my_share, share), :],
                ex_send.at[base + 2 * g + 1, k], ex_recv.at[base + 2 * g + 1, k],
                device_id={"ctx": to}, device_id_type=MESH,
            )

        return first, second

    def beside(i, src, dst, k):
        return pltpu.make_async_remote_copy(
            src, dst, be_send.at[i, k], be_recv.at[i, k],
            device_id={"ctx": wrap(me + k, n)}, device_id_type=MESH,
        )

    def fade_copy(g, k):
        return beside(g, own_f.at[g], got_f.at[me, g], k)

    def sums_copy(k):
        return beside(groups, sums_v, got_p.at[me], k)

    def send_shares(copies, g, state, got, fades):
        for k in range(1, n):
            def _(k=k):
                if fades:
                    fade_copy(g, k).start()
                copies[0](k).start()
            when(holds(wrap(me + k, n)), _)

        def _():
            got[pl.ds(me, 1), g] = state[g, pl.ds(my_share, share), :][None]
            if fades:
                got_f[pl.ds(me, 1), g] = own_f[g][None]
        when(is_holder, _)

    def carry_shares(copies, g, got, result, into, reverse):
        first, second = copies

        def _():
            for k in range(1, n):
                if not reverse:
                    fade_copy(g, k).wait_recv()
                first(k).wait_recv()
            carried = jnp.zeros((share, width), F32)
            for d in reversed(range(n)) if reverse else range(n):
                result[d, g] = carried.astype(BF16)
                carried = got_f[d, g] * carried + got[d, g].astype(F32)
            for k in range(1, n):
                second(k).start()
            into[g, pl.ds(my_share, share), :] = result[me, g]
        when(is_holder, _)

    def take_shares(copies):
        for k in range(1, n):
            def _(k=k):
                copies[1](k).wait_recv()
            when(holds(wrap(me - k, n)), _)

    def drain_shares(copies, g, fades):
        for k in range(1, n):
            def _(k=k):
                if fades:
                    fade_copy(g, k).wait_send()
                copies[0](k).wait_send()
            when(holds(wrap(me + k, n)), _)
            def _(k=k):
                copies[1](k).wait_send()
            when(is_holder, _)

    def at(c):
        return slice(c * CHUNK, (c + 1) * CHUNK)

    def wide(g):
        return slice(g * width, (g + 1) * width)

    def narrow(g):
        return slice(g * N, (g + 1) * N)

    left = lax.broadcasted_iota(jnp.int32, (CHUNK, 128), 1) < P_SIZE

    def local_state(g):
        state = jnp.zeros((N, width), F32)
        decay = jnp.ones((1, width), F32)
        for c in range(spans):
            row, col = cumulated(log_v[g * heads : (g + 1) * heads, at(c)])
            i = g * spans + c
            row_t[i] = row
            col_t[i] = col
            col = col[:, :heads]
            from_start = spread(jnp.exp(col), width)
            to_closing = spread(jnp.exp(col[-1:, :] - col), width)
            start_t[i] = from_start
            close_t[i] = to_closing
            span = from_start[-1:, :]
            scaled = (x_v[at(c), wide(g)].astype(F32) * to_closing).astype(BF16)
            state = state * span + mm(b_v[at(c), narrow(g)], scaled, TN)
            decay = decay * span
        own_s[g] = state.astype(BF16)
        own_f[g] = decay

    def intra(g, c):
        i = g * spans + c
        row, col = row_t[i], col_t[i]
        lower = (
            lax.broadcasted_iota(jnp.int32, (CHUNK, CHUNK), 0)
            >= lax.broadcasted_iota(jnp.int32, (CHUNK, CHUNK), 1)
        )
        x = x_v[at(c), wide(g)]
        inner = mm(c_v[at(c), narrow(g)], b_v[at(c), narrow(g)], NT)
        for k in range(width // 128):
            two = x[:, 128 * k : 128 * k + 128]
            parts = []
            for h in (2 * k, 2 * k + 1):
                gap = jnp.where(lower, col[:, h : h + 1] - row[h : h + 1, :], -1e30)
                parts.append(mm((jnp.exp(gap) * inner).astype(BF16), two))
            lanes = slice(g * width + 128 * k, g * width + 128 * k + 128)
            core_v[at(c), lanes] = jnp.where(left, parts[0], parts[1])

    def norm_copy(g):
        return pltpu.make_async_remote_copy(
            normed_v.at[g, other], other_n.at[g], norm_send.at[g], norm_recv.at[g],
            device_id={"ctx": pair}, device_id_type=MESH,
        )

    def forward(g):
        state = arriving[g].astype(F32)
        for c in range(spans):
            i = g * spans + c
            entry = state.astype(BF16)
            entry_v[i] = entry
            xf = x_v[at(c), wide(g)].astype(F32)
            from_start = start_t[i]
            core_now = core_v[at(c), wide(g)] + from_start * mm(c_v[at(c), narrow(g)], entry)
            core_v[at(c), wide(g)] = core_now
            y = core_now + skip_ref[:, wide(g)] * xf
            z = z_v[at(c), wide(g)].astype(F32)
            gated = y * (z * jax.nn.sigmoid(z))
            inv = lax.rsqrt(jnp.mean(gated * gated, axis=1, keepdims=True) + 1e-05)
            normed = (gated * inv * gain_ref[:, wide(g)]).astype(BF16)
            normed_v[g, 0, at(c), :] = normed[:, :half_w]
            normed_v[g, 1, at(c), :] = normed[:, half_w:]
            if c < spans - 1:
                scaled = (xf * close_t[i]).astype(BF16)
                state = state * from_start[-1:, :] + mm(b_v[at(c), narrow(g)], scaled, TN)
        norm_copy(g).start()
        trans_n[g, :, pl.ds(pl.multiple_of(side * tokens, CHUNK), tokens)] = jnp.transpose(
            normed_v[g, side]
        )

    def middle(g, c):
        i = g * spans + c
        from_start = start_t[i]
        gain = gain_ref[:, wide(g)]
        dn = mm(rows_v[side, at(c), :], w_v[wide(g), :], NT).astype(BF16).astype(F32)
        xf = x_v[at(c), wide(g)].astype(F32)
        z = z_v[at(c), wide(g)].astype(F32)
        y = core_v[at(c), wide(g)] + skip_ref[:, wide(g)] * xf
        s = jax.nn.sigmoid(z)
        silu = z * s
        gated = y * silu
        inv = lax.rsqrt(jnp.mean(gated * gated, axis=1, keepdims=True) + 1e-05)
        gain_sum = jnp.sum(dn * gated * inv, axis=0, keepdims=True)
        scaled = gain * dn
        mean = jnp.mean(scaled * gated, axis=1, keepdims=True)
        dgated = inv * scaled - gated * (inv * inv * inv * mean)
        gate_v[at(c), wide(g)] = dgated * y * s * (1.0 + z * (1.0 - s))
        dy = dgated * silu
        dy_v[at(c), wide(g)] = dy
        skip_sum = jnp.sum(dy * xf, axis=0, keepdims=True)
        flow = mm(c_v[at(c), narrow(g)], (dy * from_start).astype(BF16), TN)
        if c == spans - 1:
            sums_v[g : g + 1, :] = gain_sum
            sums_v[groups + g : groups + g + 1, :] = skip_sum
            out_flow[g] = flow
        else:
            sums_v[g : g + 1, :] += gain_sum
            sums_v[groups + g : groups + g + 1, :] += skip_sum
            out_flow[g] = out_flow[g] * from_start[-1:, :] + flow
        if c == 0:
            own_l[g] = out_flow[g].astype(BF16)

    def layer_terms(j):
        cut = slice(j * 512, (j + 1) * 512)
        total = jnp.zeros((tokens, 512), F32)
        for g in range(groups):
            both = jnp.concatenate([normed_v[g, 0], normed_v[g, 1]], axis=1)
            total += mm(both, w_v[wide(g), cut])
        layer_part[:, cut] = total.astype(BF16)

    def layer_copy(k):
        to = wrap(hd + k, nh)
        return pltpu.make_async_remote_copy(
            layer_part.at[pl.ds(pl.multiple_of(to * block, 16), block), :], layer_got.at[k - 1],
            lay_send.at[k - 1], lay_recv.at[k - 1], device_id={"head": to}, device_id_type=MESH,
        )

    def layer_sum():
        total = layer_part[pl.ds(pl.multiple_of(hd * block, 16), block), :].astype(F32)
        for k in range(1, nh):
            layer_copy(k).wait_recv()
            total += layer_got[k - 1].astype(F32)
        layer_v[...] = total.astype(BF16)

    def back_inner(g, c):
        i = g * spans + c
        row, col = row_t[i], col_t[i]
        upper = (
            lax.broadcasted_iota(jnp.int32, (CHUNK, CHUNK), 0)
            <= lax.broadcasted_iota(jnp.int32, (CHUNK, CHUNK), 1)
        )
        x = x_v[at(c), wide(g)]
        xf = x.astype(F32)
        dyf = dy_v[at(c), wide(g)]
        dy = dyf.astype(BF16)
        bm, cm = b_v[at(c), narrow(g)], c_v[at(c), narrow(g)]
        inner = mm(bm, cm, NT)
        pair_sum = jnp.zeros((CHUNK, CHUNK), F32)
        for k in range(width // 128):
            cut = slice(128 * k, 128 * k + 128)
            x_two, dy_two = xf[:, cut], dy[:, cut]
            parts = []
            for h, lanes in ((2 * k, left), (2 * k + 1, ~left)):
                gap = jnp.where(upper, row[h : h + 1, :] - col[:, h : h + 1], -1e30)
                fade = jnp.exp(gap)
                parts.append(mm((fade * inner).astype(BF16), dy_two))
                one = jnp.where(lanes, x_two, 0.0).astype(BF16)
                pair_sum += mm(one, dy_two, NT) * fade
            lanes = slice(g * width + 128 * k, g * width + 128 * k + 128)
            signal_v[at(c), lanes] = jnp.where(left, parts[0], parts[1])
        pair_sum = pair_sum.astype(BF16)
        map_v[at(c), narrow(g)] = mm(pair_sum, cm)
        dy_start = (dyf * start_t[i]).astype(BF16)
        read_v[at(c), narrow(g)] = mm(pair_sum, bm, TN) + mm(dy_start, entry_v[i], NT)

    def back_outer(g):
        own = (
            lax.broadcasted_iota(jnp.int32, (heads, width), 1) // P_SIZE
            == lax.broadcasted_iota(jnp.int32, (heads, width), 0)
        )
        own = jnp.where(own, 1.0, 0.0).astype(BF16)
        flow = arriving_l[g].astype(F32)
        for c in reversed(range(spans)):
            i = g * spans + c
            out = flow.astype(BF16)
            xf = x_v[at(c), wide(g)].astype(F32)
            dyf = dy_v[at(c), wide(g)]
            to_closing = close_t[i]
            core_grad = signal_v[at(c), wide(g)] + to_closing * mm(b_v[at(c), narrow(g)], out)
            signal_v[at(c), wide(g)] = core_grad + skip_ref[:, wide(g)] * dyf
            map_v[at(c), narrow(g)] += mm((xf * to_closing).astype(BF16), out, NT)
            slope = dyf * core_v[at(c), wide(g)] - xf * core_grad
            hi = slope.astype(BF16)
            low = (slope - hi.astype(F32)).astype(BF16)
            decay_v[g * heads : (g + 1) * heads, at(c)] = mm(own, hi, NT) + mm(own, low, NT)
            if c > 0:
                from_start = start_t[i]
                dy_start = (dyf * from_start).astype(BF16)
                flow = flow * from_start[-1:, :] + mm(c_v[at(c), narrow(g)], dy_start, TN)

    pieces = [(g, j) for g in range(groups) for j in range(cols)]
    below, above, here = at_line < root, at_line > root, at_line == root
    first_end, last_end = at_line == 0, at_line == line - 1
    lower_id, upper_id = wrap(me - 2, n), wrap(me + 2, n)

    def remote(src, dst, send, recv, to):
        return pltpu.make_async_remote_copy(
            src, dst, send, recv, device_id={"ctx": to}, device_id_type=MESH
        )

    def term_up(i):
        return remote(stage.at[i], from_left.at[i], line_send.at[i], left_recv.at[i], upper_id)

    def term_down(i):
        return remote(stage.at[i], from_right.at[i], line_send.at[i], right_recv.at[i], lower_id)

    def fin_at(i, which):
        return fin.at[i // cols, which, lax.rem(i, cols)]

    def fin_down(i):
        return remote(fin_at(i, side), fin_at(i, side), fin_left.at[i], fin_recv.at[i], lower_id)

    def fin_up(i):
        return remote(fin_at(i, side), fin_at(i, side), fin_right.at[i], fin_recv.at[i], upper_id)

    def fin_side(i):
        return remote(fin_at(i, side), fin_at(i, side), side_send.at[i], side_recv.at[i], pair)

    def fin_side_in(i):
        return remote(fin_at(i, other), fin_at(i, other), side_send.at[i], side_recv.at[i], pair)

    def reduce_piece(i):
        g, j = pieces[i]
        if j == 0:
            norm_copy(g).wait_recv()
            trans_n[g, :, pl.ds(pl.multiple_of(other * tokens, CHUNK), tokens)] = jnp.transpose(
                other_n[g]
            )
        cut = slice(j * PIECE, (j + 1) * PIECE)
        own = mm(trans_n[g, :, :tokens], rows_v[0, :, cut])
        own += mm(trans_n[g, :, tokens:], rows_v[1, :, cut])

        @pl.when(below)
        def _():
            @pl.when(first_end)
            def _():
                stage[i] = own.astype(BF16)

            @pl.when(jnp.logical_not(first_end))
            def _():
                term_up(i).wait_recv()
                stage[i] = (own + from_left[i].astype(F32)).astype(BF16)

            term_up(i).start()

        @pl.when(above)
        def _():
            @pl.when(last_end)
            def _():
                stage[i] = own.astype(BF16)

            @pl.when(jnp.logical_not(last_end))
            def _():
                term_down(i).wait_recv()
                stage[i] = (own + from_right[i].astype(F32)).astype(BF16)

            term_down(i).start()

        @pl.when(here)
        def _():
            total = own
            if root > 0:
                term_up(i).wait_recv()
                total += from_left[i].astype(F32)
            if root < line - 1:
                term_down(i).wait_recv()
                total += from_right[i].astype(F32)
            fin[g, pl.ds(side, 1), j] = total.astype(BF16)[None]
            if root > 0:
                fin_down(i).start()
            if root < line - 1:
                fin_up(i).start()
            fin_side(i).start()

    def pass_on(i):
        @pl.when(jnp.logical_not(here))
        def _():
            fin_up(i).wait_recv()

            @pl.when(jnp.logical_and(below, jnp.logical_not(first_end)))
            def _():
                fin_down(i).start()

            @pl.when(jnp.logical_and(above, jnp.logical_not(last_end)))
            def _():
                fin_up(i).start()

            fin_side(i).start()

    def take_side(i):
        fin_side_in(i).wait_recv()

    def drain_piece(i):
        @pl.when(jnp.logical_not(here))
        def _():
            term_up(i).wait_send()

        goes_down = jnp.logical_or(
            jnp.logical_and(here, jnp.logical_not(first_end)),
            jnp.logical_and(below, jnp.logical_not(first_end)),
        )
        goes_up = jnp.logical_or(
            jnp.logical_and(here, jnp.logical_not(last_end)),
            jnp.logical_and(above, jnp.logical_not(last_end)),
        )

        @pl.when(goes_down)
        def _():
            fin_down(i).wait_send()

        @pl.when(goes_up)
        def _():
            fin_up(i).wait_send()

        fin_side(i).wait_send()

    ex_f = [exchange(0, g, own_s, got_s, turned, arriving) for g in range(groups)]
    ex_b = [exchange(2 * groups, g, own_l, got_l, turned_l, arriving_l) for g in range(groups)]

    ones = lax.broadcasted_iota(jnp.int32, (1, 128), 1) < P_SIZE
    for k in range(groups * width // 128):
        skip_ref[:, 128 * k : 128 * k + 128] = jnp.where(ones, skip_s[2 * k], skip_s[2 * k + 1])

    for i in (0, 1, 2):
        loads[i].wait()
    for load in loads[3:]:
        load.start()
    for g in range(groups):
        local_state(g)
        send_shares(ex_f[g], g, own_s, got_s, True)
    rows_side(0)
    loads[3].wait()
    todo = [(g, c) for g in range(groups) for c in range(spans)]
    intra(*todo[0])
    for g in range(groups):
        carry_shares(ex_f[g], g, got_s, turned, arriving, False)
        intra(*todo[1 + g])
    rows_side(1)
    loads[4].wait()
    take_shares(ex_f[0])
    forward(0)
    rows_near(0)
    rows_relay(0)
    for one in todo[1 + groups :]:
        intra(*one)
    for g in range(1, groups):
        take_shares(ex_f[g])
        forward(g)
    rows_near(1)
    rows_relay(1)
    rows_end(0)
    rows_last(0)
    loads[5].wait()

    def rows_full():
        rows_end(1)
        rows_last(1)

    def start_layer():
        for k in range(1, nh):
            layer_copy(k).start()

    def later_send(g):
        send_shares(ex_b[g], g, own_l, got_l, False)

    def sums_send():
        for k in range(1, n):
            sums_copy(k).start()
        got_p[pl.ds(me, 1)] = sums_v[...][None]

    def later_carry(g):
        carry_shares(ex_b[g], g, got_l, turned_l, arriving_l, True)

    def params_sum():
        for k in range(1, n):
            sums_copy(k).wait_recv()
        total = jnp.zeros((2 * groups, width), F32)
        for d in range(n):
            total += got_p[d]
        lane = lax.broadcasted_iota(jnp.int32, (1, width), 1) // P_SIZE
        spot = lax.broadcasted_iota(jnp.int32, (1, groups * heads), 1)
        found = jnp.zeros((1, groups * heads), F32)
        for g in range(groups):
            gain_out[:, wide(g)] = total[g : g + 1]
            row = total[groups + g : groups + g + 1]
            for h in range(heads):
                head = jnp.sum(jnp.where(lane == h, row, 0.0), axis=1, keepdims=True)
                found = jnp.where(spot == g * heads + h, head, found)
        skip_out[...] = found

    items = [partial(layer_terms, j) for j in range(model // 512)]
    items += [start_layer]
    for g in range(groups):
        items += [partial(middle, g, c) for c in reversed(range(spans))]
        items += [partial(later_send, g)]
    items += [sums_send]
    inner_items = [partial(back_inner, g, c) for g in range(groups) for c in range(spans)]
    items += inner_items[: len(inner_items) // 2]
    items += [partial(later_carry, g) for g in range(groups)]
    items += inner_items[len(inner_items) // 2 :]
    for g in range(groups):
        items += [partial(take_shares, ex_b[g]), partial(back_outer, g)]
    items += [params_sum, layer_sum]

    count = len(pieces)
    lag = jnp.where(here, 0, LAG + LAG_HOP * (jnp.abs(at_line - root) - 1))
    max_lag = LAG + LAG_HOP * (max(root, line - 1 - root) - 1)
    ticks = count + max_lag + LAG_SIDE
    done = 0
    for t in range(ticks):
        if t == cols // 2 - 1:
            rows_full()
        if t < count:
            reduce_piece(t)

        @pl.when(jnp.logical_and(t - lag >= 0, t - lag < count))
        def _():
            pass_on(t - lag)

        late = t - lag - LAG_SIDE

        @pl.when(jnp.logical_and(late >= 0, late < count))
        def _():
            take_side(late)

        want = min(len(items) * (t + 1) // count, len(items))
        while done < want:
            items[done]()
            done += 1

    for q in range(2):
        for kind, k in row_all:
            row_copy(q, kind, k).wait_send()
    for g in range(groups):
        drain_shares(ex_f[g], g, True)
        drain_shares(ex_b[g], g, False)
    for k in range(1, n):
        sums_copy(k).wait_send()
    for g in range(groups):
        norm_copy(g).wait_send()
    for k in range(1, nh):
        layer_copy(k).wait_send()
    for i in range(count):
        drain_piece(jnp.int32(i))


def finish_kernel(
    layer_in, signal_in, gate_in, map_in, read_in, decay_in, gain_in, skip_in, weight_in,
    layer_out, signal_out, gate_out, map_out, read_out, decay_out, gain_out, skip_out, weight_out,
    wide_v, sem, weight_sem,
):
    groups, sides, cols, half_w, _ = weight_in.shape
    pairs = [
        (signal_in, signal_out), (gate_in, gate_out), (map_in, map_out), (read_in, read_out),
        (layer_in, layer_out), (decay_in, decay_out), (gain_in, gain_out), (skip_in, skip_out),
    ]
    copies = [pltpu.make_async_copy(a, b, sem.at[i]) for i, (a, b) in enumerate(pairs)]
    for copy in copies:
        copy.start()
    for g in range(groups):
        for s in range(sides):
            i = g * sides + s
            for j in range(cols):
                wide_v[i, :, j * PIECE : (j + 1) * PIECE] = weight_in[g, s, j].astype(F32)
            copy = pltpu.make_async_copy(
                wide_v.at[i], weight_out.at[pl.ds(i * half_w, half_w), :], weight_sem.at[i]
            )
            copy.start()
            copies.append(copy)
    for copy in copies:
        copy.wait()


def on_device(
    n, nh,
    signal, gate_input, input_map, readout, log_decay, skip_gain, norm_gain, out_weight, out_grad,
):
    tokens, features = signal.shape
    heads = log_decay.shape[0]
    groups = input_map.shape[1] // N
    width = features // groups
    model = out_weight.shape[1]
    block = out_grad.shape[0]
    spans = tokens // CHUNK
    cols = model // PIECE
    count = groups * cols
    half_w = width // 2
    chips = nh // 2
    sds = jax.ShapeDtypeStruct
    vm = pltpu.VMEM
    dma = pltpu.SemaphoreType.DMA

    gain = norm_gain.reshape(1, features)
    hbm = pl.BlockSpec(memory_space=pl.ANY)
    near = pl.BlockSpec(memory_space=pltpu.VMEM)
    sizes = (n, nh, tokens, groups, width, model)
    kinds = 3 + 4 * (chips - 1)
    all_spans = groups * spans
    results = [
        ((block, model), BF16),
        ((tokens, features), F32),
        ((tokens, features), F32),
        ((tokens, groups * N), F32),
        ((tokens, groups * N), F32),
        ((heads, tokens), F32),
        ((1, features), F32),
        ((1, heads), F32),
        ((groups, 2, cols, half_w, PIECE), BF16),
    ]
    held = pl.pallas_call(
        partial(layer_kernel, sizes),
        in_specs=[hbm] * 7 + [pl.BlockSpec(memory_space=pltpu.SMEM), near],
        out_specs=[near] * 9,
        out_shape=[pltpu.VMEM(shape, dtype) for shape, dtype in results],
        scratch_shapes=[
            vm((tokens, features), BF16), vm((tokens, features), BF16),
            vm((tokens, groups * N), BF16), vm((tokens, groups * N), BF16),
            vm((heads, tokens), F32), vm((features, model), BF16), vm((2, tokens, model), BF16),
            vm((all_spans, heads // groups, CHUNK), F32), vm((all_spans, CHUNK, 128), F32),
            vm((all_spans, CHUNK, width), F32), vm((all_spans, CHUNK, width), F32),
            vm((groups, N, width), BF16), vm((groups, 1, width), F32),
            vm((n, groups, 16, width), BF16), vm((n, groups, 1, width), F32),
            vm((n, groups, 16, width), BF16), vm((groups, N, width), BF16),
            vm((tokens, features), F32), vm((all_spans, N, width), BF16),
            vm((groups, 2, tokens, half_w), BF16), vm((groups, tokens, half_w), BF16),
            vm((groups, half_w, 2 * tokens), BF16),
            vm((tokens, features), F32), vm((1, features), F32),
            vm((groups, N, width), F32), vm((groups, N, width), BF16),
            vm((n, groups, 16, width), BF16), vm((n, groups, 16, width), BF16),
            vm((groups, N, width), BF16),
            vm((2 * groups, width), F32), vm((n, 2 * groups, width), F32),
            vm((tokens, model), BF16), vm((nh - 1, block, model), BF16),
            vm((count, half_w, PIECE), BF16), vm((count, half_w, PIECE), BF16),
            vm((count, half_w, PIECE), BF16),
            dma((6,)), dma((2,)),
            dma((2, kinds)), dma((2, kinds)), dma((4 * groups, n)), dma((4 * groups, n)),
            dma((groups + 1, n)), dma((groups + 1, n)),
            dma((groups,)), dma((groups,)), dma((nh - 1,)), dma((nh - 1,)),
            dma((count,)), dma((count,)), dma((count,)), dma((count,)), dma((count,)), dma((count,)),
            dma((count,)), dma((count,)),
        ],
        compiler_params=pltpu.CompilerParams(
            collective_id=0, has_side_effects=True, vmem_limit_bytes=VMEM_LIMIT
        ),
        name="layer",
    )(signal, gate_input, input_map, readout, log_decay, out_weight, out_grad, skip_gain, gain)

    results[-1] = ((features, model), F32)
    outs = pl.pallas_call(
        finish_kernel,
        in_specs=[near] * 9,
        out_specs=[hbm] * 9,
        out_shape=[sds(shape, dtype) for shape, dtype in results],
        scratch_shapes=[vm((2 * groups, half_w, model), F32), dma((8,)), dma((2 * groups,))],
        compiler_params=pltpu.CompilerParams(vmem_limit_bytes=24 * 1024 * 1024),
        name="finish",
    )(*held)
    layer_out, signal_grad, gate_grad, map_grad, read_grad, decay_grad, gain, skip, weight = outs
    return (
        layer_out, signal_grad, gate_grad, map_grad, read_grad, decay_grad,
        skip.reshape(heads), gain.reshape(features), weight,
    )


def solution(mesh):
    return jax.shard_map(
        partial(on_device, mesh.shape["ctx"], mesh.shape["head"]),
        mesh=mesh,
        in_specs=(
            P("ctx", "head"),
            P("ctx", "head"),
            P("ctx", "head"),
            P("ctx", "head"),
            P("head", "ctx"),
            P("head"),
            P("head"),
            P("head", None),
            P(("ctx", "head"), None),
        ),
        out_specs=(
            P(("ctx", "head"), None),
            P("ctx", "head"),
            P("ctx", "head"),
            P("ctx", "head"),
            P("ctx", "head"),
            P("head", "ctx"),
            P("head"),
            P("head"),
            P("head", None),
        ),
        check_vma=False,
    )
```

```python
from functools import partial

import jax
import jax.numpy as jnp
from jax import lax
from jax.experimental import pallas as pl
from jax.experimental.pallas import tpu as pltpu
from jax.sharding import PartitionSpec as P

P_SIZE = 64
N = 128
CHUNK = 256
PIECE = 128
LAG = 6
LAG_HOP = 4
LAG_SIDE = 4
F32 = jnp.float32
BF16 = jnp.bfloat16
VMEM_LIMIT = 46 * 1024 * 1024
MESH = pl.DeviceIdType.MESH

NN = (((1,), (0,)), ((), ()))
NT = (((1,), (1,)), ((), ()))
TN = (((0,), (0,)), ((), ()))


def mm(a, b, dims=NN):
    return lax.dot_general(a, b, dims, preferred_element_type=F32)


def spread(factor, width):
    rows = factor.shape[0]
    left = lax.broadcasted_iota(jnp.int32, (rows, 128), 1) < P_SIZE
    pairs = []
    for k in range(width // 128):
        a = jnp.broadcast_to(factor[:, 2 * k : 2 * k + 1], (rows, 128))
        b = jnp.broadcast_to(factor[:, 2 * k + 1 : 2 * k + 2], (rows, 128))
        pairs.append(jnp.where(left, a, b))
    return jnp.concatenate(pairs, axis=1)


def cumulated(log_row):
    heads, length = log_row.shape
    hi = log_row.astype(BF16).astype(F32)
    rest = log_row - hi
    mid = rest.astype(BF16).astype(F32)
    low = rest - mid
    parts = jnp.concatenate([hi, mid, low, jnp.zeros_like(hi)], axis=0).astype(BF16)
    upper = (
        lax.broadcasted_iota(jnp.int32, (length, length), 0)
        <= lax.broadcasted_iota(jnp.int32, (length, length), 1)
    )
    sums = mm(parts, jnp.where(upper, 1.0, 0.0).astype(BF16))
    row = sums[0:heads] + sums[heads : 2 * heads] + sums[2 * heads : 3 * heads]
    col = jnp.transpose(jnp.concatenate([row] * (128 // heads), axis=0))
    return row, col


def layer_kernel(
    sizes,
    x_hbm, z_hbm, b_hbm, c_hbm, log_hbm, w_hbm, og_hbm, skip_s, gain_ref,
    layer_v, signal_v, gate_v, map_v, read_v, decay_v, gain_out, skip_out, fin,
    x_v, z_v, b_v, c_v, log_v, w_v, rows_v,
    row_t, col_t, start_t, close_t,
    own_s, own_f, got_s, got_f, turned, arriving,
    core_v, entry_v, normed_v, other_n, trans_n,
    dy_v, dn_v, skip_ref,
    out_flow, own_l, got_l, turned_l, arriving_l, sums_v, got_p,
    layer_part, layer_got,
    stage, from_left, from_right,
    in_sem, own_row_sem,
    row_send, row_recv, ex_send, ex_recv, be_send, be_recv, norm_send, norm_recv, lay_send, lay_recv,
    line_send, left_recv, right_recv, fin_left, fin_right, fin_recv, side_send, side_recv,
):
    n, nh, tokens, groups, width, model = sizes
    spans = tokens // CHUNK
    half_w = width // 2
    heads = width // P_SIZE
    block = og_hbm.shape[0]
    share = 16
    holders = N // share
    stride = max(1, n // holders)
    line = n // 2
    root = (line - 1) // 2
    cols = model // PIECE
    halves = model // 2

    me = lax.axis_index("ctx")
    hd = lax.axis_index("head")
    side = lax.rem(me, 2)
    other = 1 - side
    pair = me + 1 - 2 * side
    at_line = me // 2
    core = lax.rem(hd, 2)
    sibling = hd + 1 - 2 * core

    def wrap(i, size):
        return lax.rem(i + size, size)

    def when(cond, fn):
        if cond is True:
            fn()
        else:
            pl.when(cond)(fn)

    inputs = [
        (log_hbm, log_v), (b_hbm, b_v), (x_hbm, x_v), (c_hbm, c_v), (z_hbm, z_v), (w_hbm, w_v),
    ]
    loads = [pltpu.make_async_copy(a, b, in_sem.at[i]) for i, (a, b) in enumerate(inputs)]
    for load in loads[:3]:
        load.start()

    def row_at(which, head, q):
        at = pl.ds(pl.multiple_of(head * block, 16), block)
        return rows_v.at[which, at, pl.ds(q * halves, halves)]

    own_rows = [
        pltpu.make_async_copy(
            og_hbm.at[:, pl.ds(q * halves, halves)], row_at(side, hd, q), own_row_sem.at[q]
        )
        for q in range(2)
    ]
    for copy in own_rows:
        copy.start()

    barrier = pltpu.get_barrier_semaphore()
    for k in range(1, n):
        pl.semaphore_signal(
            barrier, inc=1, device_id={"ctx": wrap(me + k, n)}, device_id_type=MESH
        )
    for k in range(1, nh):
        pl.semaphore_signal(
            barrier, inc=1, device_id={"head": wrap(hd + k, nh)}, device_id_type=MESH
        )
    pl.semaphore_wait(barrier, n - 1 + nh - 1)

    chips = nh // 2

    def row_copy(q, kind, k):
        x_next = wrap(hd + 2 * k, nh)
        x_from = wrap(hd - 2 * k, nh)
        if kind in ("x", "sib", "side"):
            src = og_hbm.at[:, pl.ds(q * halves, halves)]
            dst = row_at(side, hd, q)
        elif kind == "x_sib":
            src = dst = row_at(side, x_from, q)
        elif kind in ("side_sib", "side_x"):
            src = dst = row_at(other, hd, q)
        else:
            src = dst = row_at(other, x_from, q)
        if kind in ("x", "side_x"):
            target = {"head": x_next}
        elif kind == "side":
            target = {"ctx": pair}
        else:
            target = {"head": sibling}
        i = {"sib": 0, "side": 1, "side_sib": 2}.get(kind)
        if i is None:
            i = 3 + {"x": 0, "x_sib": 1, "side_x": 2, "side_x_sib": 3}[kind] * (chips - 1) + k - 1
        return pltpu.make_async_remote_copy(
            src, dst, row_send.at[q, i], row_recv.at[q, i], device_id=target, device_id_type=MESH
        )

    away = range(1, chips)
    row_all = [("sib", 0), ("side", 0), ("side_sib", 0)]
    row_all += [(kind, k) for kind in ("x", "x_sib", "side_x", "side_x_sib") for k in away]
    for q in range(2):
        for k in away:
            row_copy(q, "x", k).start()
        if q == 0:
            row_copy(q, "side", 0).start()
        row_copy(q, "sib", 0).start()

    def rows_side(q):
        row_copy(q, "side", 0).start()

    def rows_relay(q):
        row_copy(q, "side", 0).wait_recv()
        for k in away:
            row_copy(q, "side_x", k).start()
        row_copy(q, "side_sib", 0).start()

    def rows_near(q):
        for k in away:
            row_copy(q, "x", k).wait_recv()
            row_copy(q, "x_sib", k).start()

    def rows_end(q):
        for k in away:
            row_copy(q, "side_x", k).wait_recv()
            row_copy(q, "side_x_sib", k).start()

    def rows_own(q):
        row_copy(q, "sib", 0).wait_recv()
        own_rows[q].wait()
        for k in away:
            row_copy(q, "x_sib", k).wait_recv()

    def rows_last(q):
        row_copy(q, "side_sib", 0).wait_recv()
        for k in away:
            row_copy(q, "side_x_sib", k).wait_recv()

    is_holder = True if stride == 1 else lax.rem(me, stride) == 0
    my_share = pl.multiple_of(me // stride * share, share)

    def holds(i):
        return True if stride == 1 else lax.rem(i, stride) == 0

    def exchange(base, g, state, got, result, into):
        def first(k):
            to = wrap(me + k, n)
            part = pl.ds(pl.multiple_of(to // stride * share, share), share)
            return pltpu.make_async_remote_copy(
                state.at[g, part, :], got.at[me, g],
                ex_send.at[base + 2 * g, k], ex_recv.at[base + 2 * g, k],
                device_id={"ctx": to}, device_id_type=MESH,
            )

        def second(k):
            to = wrap(me + k, n)
            return pltpu.make_async_remote_copy(
                result.at[to, g], into.at[g, pl.ds(my_share, share), :],
                ex_send.at[base + 2 * g + 1, k], ex_recv.at[base + 2 * g + 1, k],
                device_id={"ctx": to}, device_id_type=MESH,
            )

        return first, second

    def beside(i, src, dst, k):
        return pltpu.make_async_remote_copy(
            src, dst, be_send.at[i, k], be_recv.at[i, k],
            device_id={"ctx": wrap(me + k, n)}, device_id_type=MESH,
        )

    def fade_copy(g, k):
        return beside(g, own_f.at[g], got_f.at[me, g], k)

    def sums_copy(k):
        return beside(groups, sums_v, got_p.at[me], k)

    def send_shares(copies, g, state, got, fades):
        for k in range(1, n):
            def _(k=k):
                if fades:
                    fade_copy(g, k).start()
                copies[0](k).start()
            when(holds(wrap(me + k, n)), _)

        def _():
            got[pl.ds(me, 1), g] = state[g, pl.ds(my_share, share), :][None]
            if fades:
                got_f[pl.ds(me, 1), g] = own_f[g][None]
        when(is_holder, _)

    def carry_shares(copies, g, got, result, into, reverse):
        first, second = copies

        def _():
            for k in range(1, n):
                if not reverse:
                    fade_copy(g, k).wait_recv()
                first(k).wait_recv()
            carried = jnp.zeros((share, width), F32)
            for d in reversed(range(n)) if reverse else range(n):
                result[d, g] = carried.astype(BF16)
                carried = got_f[d, g] * carried + got[d, g].astype(F32)
            for k in range(1, n):
                second(k).start()
            into[g, pl.ds(my_share, share), :] = result[me, g]
        when(is_holder, _)

    def take_shares(copies):
        for k in range(1, n):
            def _(k=k):
                copies[1](k).wait_recv()
            when(holds(wrap(me - k, n)), _)

    def drain_shares(copies, g, fades):
        for k in range(1, n):
            def _(k=k):
                if fades:
                    fade_copy(g, k).wait_send()
                copies[0](k).wait_send()
            when(holds(wrap(me + k, n)), _)
            def _(k=k):
                copies[1](k).wait_send()
            when(is_holder, _)

    def at(c):
        return slice(c * CHUNK, (c + 1) * CHUNK)

    def wide(g):
        return slice(g * width, (g + 1) * width)

    def narrow(g):
        return slice(g * N, (g + 1) * N)

    left = lax.broadcasted_iota(jnp.int32, (CHUNK, 128), 1) < P_SIZE

    def local_state(g):
        state = jnp.zeros((N, width), F32)
        decay = jnp.ones((1, width), F32)
        for c in range(spans):
            row, col = cumulated(log_v[g * heads : (g + 1) * heads, at(c)])
            i = g * spans + c
            row_t[i] = row
            col_t[i] = col
            col = col[:, :heads]
            from_start = spread(jnp.exp(col), width)
            to_closing = spread(jnp.exp(col[-1:, :] - col), width)
            start_t[i] = from_start
            close_t[i] = to_closing
            span = from_start[-1:, :]
            scaled = (x_v[at(c), wide(g)].astype(F32) * to_closing).astype(BF16)
            state = state * span + mm(b_v[at(c), narrow(g)], scaled, TN)
            decay = decay * span
        own_s[g] = state.astype(BF16)
        own_f[g] = decay

    def intra(g, c):
        i = g * spans + c
        row, col = row_t[i], col_t[i]
        lower = (
            lax.broadcasted_iota(jnp.int32, (CHUNK, CHUNK), 0)
            >= lax.broadcasted_iota(jnp.int32, (CHUNK, CHUNK), 1)
        )
        x = x_v[at(c), wide(g)]
        inner = mm(c_v[at(c), narrow(g)], b_v[at(c), narrow(g)], NT)
        for k in range(width // 128):
            two = x[:, 128 * k : 128 * k + 128]
            parts = []
            for h in (2 * k, 2 * k + 1):
                gap = jnp.where(lower, col[:, h : h + 1] - row[h : h + 1, :], -1e30)
                parts.append(mm((jnp.exp(gap) * inner).astype(BF16), two))
            lanes = slice(g * width + 128 * k, g * width + 128 * k + 128)
            core_v[at(c), lanes] = jnp.where(left, parts[0], parts[1])

    def norm_copy(g):
        return pltpu.make_async_remote_copy(
            normed_v.at[g, other], other_n.at[g], norm_send.at[g], norm_recv.at[g],
            device_id={"ctx": pair}, device_id_type=MESH,
        )

    def forward(g):
        state = arriving[g].astype(F32)
        for c in range(spans):
            i = g * spans + c
            entry = state.astype(BF16)
            entry_v[i] = entry
            xf = x_v[at(c), wide(g)].astype(F32)
            from_start = start_t[i]
            core_now = core_v[at(c), wide(g)] + from_start * mm(c_v[at(c), narrow(g)], entry)
            core_v[at(c), wide(g)] = core_now
            y = core_now + skip_ref[:, wide(g)] * xf
            z = z_v[at(c), wide(g)].astype(F32)
            gated = y * (z * jax.nn.sigmoid(z))
            inv = lax.rsqrt(jnp.mean(gated * gated, axis=1, keepdims=True) + 1e-05)
            normed = (gated * inv * gain_ref[:, wide(g)]).astype(BF16)
            normed_v[g, 0, at(c), :] = normed[:, :half_w]
            normed_v[g, 1, at(c), :] = normed[:, half_w:]
            if c < spans - 1:
                scaled = (xf * close_t[i]).astype(BF16)
                state = state * from_start[-1:, :] + mm(b_v[at(c), narrow(g)], scaled, TN)
        norm_copy(g).start()
        trans_n[g, :, pl.ds(pl.multiple_of(side * tokens, CHUNK), tokens)] = jnp.transpose(
            normed_v[g, side]
        )

    def dnormed(g, c):
        dn_v[...] = mm(rows_v[side, at(c), :], w_v[wide(g), :], NT).astype(BF16)

    def middle(g, c):
        i = g * spans + c
        from_start = start_t[i]
        gain = gain_ref[:, wide(g)]
        dn = dn_v[...].astype(F32)
        xf = x_v[at(c), wide(g)].astype(F32)
        z = z_v[at(c), wide(g)].astype(F32)
        y = core_v[at(c), wide(g)] + skip_ref[:, wide(g)] * xf
        s = jax.nn.sigmoid(z)
        silu = z * s
        gated = y * silu
        inv = lax.rsqrt(jnp.mean(gated * gated, axis=1, keepdims=True) + 1e-05)
        gain_sum = jnp.sum(dn * gated * inv, axis=0, keepdims=True)
        scaled = gain * dn
        mean = jnp.mean(scaled * gated, axis=1, keepdims=True)
        dgated = inv * scaled - gated * (inv * inv * inv * mean)
        gate_v[at(c), wide(g)] = dgated * y * s * (1.0 + z * (1.0 - s))
        dy = dgated * silu
        dy_v[at(c), wide(g)] = dy
        skip_sum = jnp.sum(dy * xf, axis=0, keepdims=True)
        flow = mm(c_v[at(c), narrow(g)], (dy * from_start).astype(BF16), TN)
        if c == spans - 1:
            sums_v[g : g + 1, :] = gain_sum
            sums_v[groups + g : groups + g + 1, :] = skip_sum
            out_flow[g] = flow
        else:
            sums_v[g : g + 1, :] += gain_sum
            sums_v[groups + g : groups + g + 1, :] += skip_sum
            out_flow[g] = out_flow[g] * from_start[-1:, :] + flow
        if c == 0:
            own_l[g] = out_flow[g].astype(BF16)

    def layer_terms(j):
        cut = slice(j * 512, (j + 1) * 512)
        total = jnp.zeros((tokens, 512), F32)
        for g in range(groups):
            both = jnp.concatenate([normed_v[g, 0], normed_v[g, 1]], axis=1)
            total += mm(both, w_v[wide(g), cut])
        layer_part[:, cut] = total.astype(BF16)

    def layer_copy(k):
        to = wrap(hd + k, nh)
        return pltpu.make_async_remote_copy(
            layer_part.at[pl.ds(pl.multiple_of(to * block, 16), block), :], layer_got.at[k - 1],
            lay_send.at[k - 1], lay_recv.at[k - 1], device_id={"head": to}, device_id_type=MESH,
        )

    def layer_sum():
        total = layer_part[pl.ds(pl.multiple_of(hd * block, 16), block), :].astype(F32)
        for k in range(1, nh):
            layer_copy(k).wait_recv()
            total += layer_got[k - 1].astype(F32)
        layer_v[...] = total.astype(BF16)

    def back_inner(g, c):
        i = g * spans + c
        row, col = row_t[i], col_t[i]
        upper = (
            lax.broadcasted_iota(jnp.int32, (CHUNK, CHUNK), 0)
            <= lax.broadcasted_iota(jnp.int32, (CHUNK, CHUNK), 1)
        )
        x = x_v[at(c), wide(g)]
        xf = x.astype(F32)
        dyf = dy_v[at(c), wide(g)]
        dy = dyf.astype(BF16)
        bm, cm = b_v[at(c), narrow(g)], c_v[at(c), narrow(g)]
        inner = mm(bm, cm, NT)
        pair_sum = jnp.zeros((CHUNK, CHUNK), F32)
        for k in range(width // 128):
            cut = slice(128 * k, 128 * k + 128)
            x_two, dy_two = xf[:, cut], dy[:, cut]
            parts = []
            for h, lanes in ((2 * k, left), (2 * k + 1, ~left)):
                gap = jnp.where(upper, row[h : h + 1, :] - col[:, h : h + 1], -1e30)
                fade = jnp.exp(gap)
                parts.append(mm((fade * inner).astype(BF16), dy_two))
                one = jnp.where(lanes, x_two, 0.0).astype(BF16)
                pair_sum += mm(one, dy_two, NT) * fade
            lanes = slice(g * width + 128 * k, g * width + 128 * k + 128)
            signal_v[at(c), lanes] = jnp.where(left, parts[0], parts[1])
        pair_sum = pair_sum.astype(BF16)
        map_v[at(c), narrow(g)] = mm(pair_sum, cm)
        dy_start = (dyf * start_t[i]).astype(BF16)
        read_v[at(c), narrow(g)] = mm(pair_sum, bm, TN) + mm(dy_start, entry_v[i], NT)

    def back_outer(g):
        own = (
            lax.broadcasted_iota(jnp.int32, (heads, width), 1) // P_SIZE
            == lax.broadcasted_iota(jnp.int32, (heads, width), 0)
        )
        own = jnp.where(own, 1.0, 0.0).astype(BF16)
        flow = arriving_l[g].astype(F32)
        for c in reversed(range(spans)):
            i = g * spans + c
            out = flow.astype(BF16)
            xf = x_v[at(c), wide(g)].astype(F32)
            dyf = dy_v[at(c), wide(g)]
            to_closing = close_t[i]
            core_grad = signal_v[at(c), wide(g)] + to_closing * mm(b_v[at(c), narrow(g)], out)
            signal_v[at(c), wide(g)] = core_grad + skip_ref[:, wide(g)] * dyf
            map_v[at(c), narrow(g)] += mm((xf * to_closing).astype(BF16), out, NT)
            slope = dyf * core_v[at(c), wide(g)] - xf * core_grad
            hi = slope.astype(BF16)
            low = (slope - hi.astype(F32)).astype(BF16)
            decay_v[g * heads : (g + 1) * heads, at(c)] = mm(own, hi, NT) + mm(own, low, NT)
            if c > 0:
                from_start = start_t[i]
                dy_start = (dyf * from_start).astype(BF16)
                flow = flow * from_start[-1:, :] + mm(c_v[at(c), narrow(g)], dy_start, TN)

    pieces = [(g, j) for g in range(groups) for j in range(cols)]
    below, above, here = at_line < root, at_line > root, at_line == root
    first_end, last_end = at_line == 0, at_line == line - 1
    lower_id, upper_id = wrap(me - 2, n), wrap(me + 2, n)

    def remote(src, dst, send, recv, to):
        return pltpu.make_async_remote_copy(
            src, dst, send, recv, device_id={"ctx": to}, device_id_type=MESH
        )

    def term_up(i):
        return remote(stage.at[i], from_left.at[i], line_send.at[i], left_recv.at[i], upper_id)

    def term_down(i):
        return remote(stage.at[i], from_right.at[i], line_send.at[i], right_recv.at[i], lower_id)

    def fin_at(i, which):
        return fin.at[i // cols, which, lax.rem(i, cols)]

    def fin_down(i):
        return remote(fin_at(i, side), fin_at(i, side), fin_left.at[i], fin_recv.at[i], lower_id)

    def fin_up(i):
        return remote(fin_at(i, side), fin_at(i, side), fin_right.at[i], fin_recv.at[i], upper_id)

    def fin_side(i):
        return remote(fin_at(i, side), fin_at(i, side), side_send.at[i], side_recv.at[i], pair)

    def fin_side_in(i):
        return remote(fin_at(i, other), fin_at(i, other), side_send.at[i], side_recv.at[i], pair)

    def reduce_piece(i):
        g, j = pieces[i]
        if j == 0:
            norm_copy(g).wait_recv()
            trans_n[g, :, pl.ds(pl.multiple_of(other * tokens, CHUNK), tokens)] = jnp.transpose(
                other_n[g]
            )
        cut = slice(j * PIECE, (j + 1) * PIECE)
        own = mm(trans_n[g, :, :tokens], rows_v[0, :, cut])
        own += mm(trans_n[g, :, tokens:], rows_v[1, :, cut])

        @pl.when(below)
        def _():
            @pl.when(first_end)
            def _():
                stage[i] = own.astype(BF16)

            @pl.when(jnp.logical_not(first_end))
            def _():
                term_up(i).wait_recv()
                stage[i] = (own + from_left[i].astype(F32)).astype(BF16)

            term_up(i).start()

        @pl.when(above)
        def _():
            @pl.when(last_end)
            def _():
                stage[i] = own.astype(BF16)

            @pl.when(jnp.logical_not(last_end))
            def _():
                term_down(i).wait_recv()
                stage[i] = (own + from_right[i].astype(F32)).astype(BF16)

            term_down(i).start()

        @pl.when(here)
        def _():
            total = own
            if root > 0:
                term_up(i).wait_recv()
                total += from_left[i].astype(F32)
            if root < line - 1:
                term_down(i).wait_recv()
                total += from_right[i].astype(F32)
            fin[g, pl.ds(side, 1), j] = total.astype(BF16)[None]
            if root > 0:
                fin_down(i).start()
            if root < line - 1:
                fin_up(i).start()
            fin_side(i).start()

    def pass_on(i):
        @pl.when(jnp.logical_not(here))
        def _():
            fin_up(i).wait_recv()

            @pl.when(jnp.logical_and(below, jnp.logical_not(first_end)))
            def _():
                fin_down(i).start()

            @pl.when(jnp.logical_and(above, jnp.logical_not(last_end)))
            def _():
                fin_up(i).start()

            fin_side(i).start()

    def take_side(i):
        fin_side_in(i).wait_recv()

    def drain_piece(i):
        @pl.when(jnp.logical_not(here))
        def _():
            term_up(i).wait_send()

        goes_down = jnp.logical_or(
            jnp.logical_and(here, jnp.logical_not(first_end)),
            jnp.logical_and(below, jnp.logical_not(first_end)),
        )
        goes_up = jnp.logical_or(
            jnp.logical_and(here, jnp.logical_not(last_end)),
            jnp.logical_and(above, jnp.logical_not(last_end)),
        )

        @pl.when(goes_down)
        def _():
            fin_down(i).wait_send()

        @pl.when(goes_up)
        def _():
            fin_up(i).wait_send()

        fin_side(i).wait_send()

    ex_f = [exchange(0, g, own_s, got_s, turned, arriving) for g in range(groups)]
    ex_b = [exchange(2 * groups, g, own_l, got_l, turned_l, arriving_l) for g in range(groups)]

    ones = lax.broadcasted_iota(jnp.int32, (1, 128), 1) < P_SIZE
    for k in range(groups * width // 128):
        skip_ref[:, 128 * k : 128 * k + 128] = jnp.where(ones, skip_s[2 * k], skip_s[2 * k + 1])

    for i in (0, 1, 2):
        loads[i].wait()
    for load in loads[3:]:
        load.start()
    for g in range(groups):
        local_state(g)
        send_shares(ex_f[g], g, own_s, got_s, True)
    loads[3].wait()
    todo = [(g, c) for g in range(groups) for c in range(spans)]
    intra(*todo[0])
    for g in range(groups):
        carry_shares(ex_f[g], g, got_s, turned, arriving, False)
        if g == 0:
            rows_near(0)
            rows_relay(0)
        intra(*todo[1 + g])
    loads[4].wait()
    take_shares(ex_f[0])
    forward(0)
    rows_side(1)
    for one in todo[1 + groups :]:
        intra(*one)
    rows_end(0)
    for g in range(1, groups):
        take_shares(ex_f[g])
        forward(g)
    rows_own(0)
    rows_last(0)
    rows_near(1)
    loads[5].wait()

    def rows_full():
        rows_end(1)
        rows_last(1)

    def start_layer():
        for k in range(1, nh):
            layer_copy(k).start()

    def later_send(g):
        send_shares(ex_b[g], g, own_l, got_l, False)

    def sums_send():
        for k in range(1, n):
            sums_copy(k).start()
        got_p[pl.ds(me, 1)] = sums_v[...][None]

    def later_carry(g):
        carry_shares(ex_b[g], g, got_l, turned_l, arriving_l, True)

    def params_sum():
        for k in range(1, n):
            sums_copy(k).wait_recv()
        total = jnp.zeros((2 * groups, width), F32)
        for d in range(n):
            total += got_p[d]
        lane = lax.broadcasted_iota(jnp.int32, (1, width), 1) // P_SIZE
        spot = lax.broadcasted_iota(jnp.int32, (1, groups * heads), 1)
        found = jnp.zeros((1, groups * heads), F32)
        for g in range(groups):
            gain_out[:, wide(g)] = total[g : g + 1]
            row = total[groups + g : groups + g + 1]
            for h in range(heads):
                head = jnp.sum(jnp.where(lane == h, row, 0.0), axis=1, keepdims=True)
                found = jnp.where(spot == g * heads + h, head, found)
        skip_out[...] = found

    items = [(0.6, partial(layer_terms, j)) for j in range(model // 512)]
    items += [(0.1, start_layer)]
    for g in range(groups):
        for c in reversed(range(spans)):
            items += [(0.8, partial(dnormed, g, c)), (2.2, partial(middle, g, c))]
        items += [(0.4, partial(later_send, g))]
    items += [(0.2, sums_send)]
    inner_items = [(2.2, partial(back_inner, g, c)) for g in range(groups) for c in range(spans)]
    items += inner_items[: len(inner_items) // 2]
    items += [(0.5, partial(later_carry, g)) for g in range(groups)]
    items += inner_items[len(inner_items) // 2 :]
    for g in range(groups):
        items += [(0.2, partial(take_shares, ex_b[g])), (1.2, partial(back_outer, g))]
    items += [(0.5, params_sum), (0.5, layer_sum)]

    count = len(pieces)
    lag = jnp.where(here, 0, LAG + LAG_HOP * (jnp.abs(at_line - root) - 1))
    max_lag = LAG + LAG_HOP * (max(root, line - 1 - root) - 1)
    ticks = count + max_lag + LAG_SIDE
    busy = count + max_lag // 2
    per_tick = sum(share for share, _ in items) / busy
    first_full = cols // 2
    spent = 0.0
    for t in range(ticks):
        if t == first_full // 4:
            rows_relay(1)
        if t == first_full:
            rows_full()
        if t < count:
            reduce_piece(t)

        @pl.when(jnp.logical_and(t - lag >= 0, t - lag < count))
        def _():
            pass_on(t - lag)

        late = t - lag - LAG_SIDE

        @pl.when(jnp.logical_and(late >= 0, late < count))
        def _():
            take_side(late)

        if t == 0:
            rows_own(1)
        while items and (spent < (t + 1) * per_tick or t + 1 >= busy):
            spent += items[0][0]
            items.pop(0)[1]()

    for q in range(2):
        for kind, k in row_all:
            row_copy(q, kind, k).wait_send()
    for g in range(groups):
        drain_shares(ex_f[g], g, True)
        drain_shares(ex_b[g], g, False)
    for k in range(1, n):
        sums_copy(k).wait_send()
    for g in range(groups):
        norm_copy(g).wait_send()
    for k in range(1, nh):
        layer_copy(k).wait_send()
    for i in range(count):
        drain_piece(jnp.int32(i))


def finish_kernel(
    layer_in, signal_in, gate_in, map_in, read_in, decay_in, gain_in, skip_in, weight_in,
    layer_out, signal_out, gate_out, map_out, read_out, decay_out, gain_out, skip_out, weight_out,
    wide_v, sem, weight_sem,
):
    groups, sides, cols, half_w, _ = weight_in.shape
    pairs = [
        (signal_in, signal_out), (gate_in, gate_out), (map_in, map_out), (read_in, read_out),
        (layer_in, layer_out), (decay_in, decay_out), (gain_in, gain_out), (skip_in, skip_out),
    ]
    copies = [pltpu.make_async_copy(a, b, sem.at[i]) for i, (a, b) in enumerate(pairs)]
    for copy in copies:
        copy.start()
    for g in range(groups):
        for s in range(sides):
            i = g * sides + s
            for j in range(cols):
                wide_v[i, :, j * PIECE : (j + 1) * PIECE] = weight_in[g, s, j].astype(F32)
            copy = pltpu.make_async_copy(
                wide_v.at[i], weight_out.at[pl.ds(i * half_w, half_w), :], weight_sem.at[i]
            )
            copy.start()
            copies.append(copy)
    for copy in copies:
        copy.wait()


def on_device(
    n, nh,
    signal, gate_input, input_map, readout, log_decay, skip_gain, norm_gain, out_weight, out_grad,
):
    tokens, features = signal.shape
    heads = log_decay.shape[0]
    groups = input_map.shape[1] // N
    width = features // groups
    model = out_weight.shape[1]
    block = out_grad.shape[0]
    spans = tokens // CHUNK
    cols = model // PIECE
    count = groups * cols
    half_w = width // 2
    chips = nh // 2
    sds = jax.ShapeDtypeStruct
    vm = pltpu.VMEM
    dma = pltpu.SemaphoreType.DMA

    gain = norm_gain.reshape(1, features)
    hbm = pl.BlockSpec(memory_space=pl.ANY)
    near = pl.BlockSpec(memory_space=pltpu.VMEM)
    sizes = (n, nh, tokens, groups, width, model)
    kinds = 3 + 4 * (chips - 1)
    all_spans = groups * spans
    results = [
        ((block, model), BF16),
        ((tokens, features), F32),
        ((tokens, features), F32),
        ((tokens, groups * N), F32),
        ((tokens, groups * N), F32),
        ((heads, tokens), F32),
        ((1, features), F32),
        ((1, heads), F32),
        ((groups, 2, cols, half_w, PIECE), BF16),
    ]
    held = pl.pallas_call(
        partial(layer_kernel, sizes),
        in_specs=[hbm] * 7 + [pl.BlockSpec(memory_space=pltpu.SMEM), near],
        out_specs=[near] * 9,
        out_shape=[pltpu.VMEM(shape, dtype) for shape, dtype in results],
        scratch_shapes=[
            vm((tokens, features), BF16), vm((tokens, features), BF16),
            vm((tokens, groups * N), BF16), vm((tokens, groups * N), BF16),
            vm((heads, tokens), F32), vm((features, model), BF16), vm((2, tokens, model), BF16),
            vm((all_spans, heads // groups, CHUNK), F32), vm((all_spans, CHUNK, 128), F32),
            vm((all_spans, CHUNK, width), F32), vm((all_spans, CHUNK, width), F32),
            vm((groups, N, width), BF16), vm((groups, 1, width), F32),
            vm((n, groups, 16, width), BF16), vm((n, groups, 1, width), F32),
            vm((n, groups, 16, width), BF16), vm((groups, N, width), BF16),
            vm((tokens, features), F32), vm((all_spans, N, width), BF16),
            vm((groups, 2, tokens, half_w), BF16), vm((groups, tokens, half_w), BF16),
            vm((groups, half_w, 2 * tokens), BF16),
            vm((tokens, features), F32), vm((CHUNK, width), BF16), vm((1, features), F32),
            vm((groups, N, width), F32), vm((groups, N, width), BF16),
            vm((n, groups, 16, width), BF16), vm((n, groups, 16, width), BF16),
            vm((groups, N, width), BF16),
            vm((2 * groups, width), F32), vm((n, 2 * groups, width), F32),
            vm((tokens, model), BF16), vm((nh - 1, block, model), BF16),
            vm((count, half_w, PIECE), BF16), vm((count, half_w, PIECE), BF16),
            vm((count, half_w, PIECE), BF16),
            dma((6,)), dma((2,)),
            dma((2, kinds)), dma((2, kinds)), dma((4 * groups, n)), dma((4 * groups, n)),
            dma((groups + 1, n)), dma((groups + 1, n)),
            dma((groups,)), dma((groups,)), dma((nh - 1,)), dma((nh - 1,)),
            dma((count,)), dma((count,)), dma((count,)), dma((count,)), dma((count,)), dma((count,)),
            dma((count,)), dma((count,)),
        ],
        compiler_params=pltpu.CompilerParams(
            collective_id=0, has_side_effects=True, vmem_limit_bytes=VMEM_LIMIT
        ),
        name="layer",
    )(signal, gate_input, input_map, readout, log_decay, out_weight, out_grad, skip_gain, gain)

    results[-1] = ((features, model), F32)
    outs = pl.pallas_call(
        finish_kernel,
        in_specs=[near] * 9,
        out_specs=[hbm] * 9,
        out_shape=[sds(shape, dtype) for shape, dtype in results],
        scratch_shapes=[vm((2 * groups, half_w, model), F32), dma((8,)), dma((2 * groups,))],
        compiler_params=pltpu.CompilerParams(vmem_limit_bytes=24 * 1024 * 1024),
        name="finish",
    )(*held)
    layer_out, signal_grad, gate_grad, map_grad, read_grad, decay_grad, gain, skip, weight = outs
    return (
        layer_out, signal_grad, gate_grad, map_grad, read_grad, decay_grad,
        skip.reshape(heads), gain.reshape(features), weight,
    )


def solution(mesh):
    return jax.shard_map(
        partial(on_device, mesh.shape["ctx"], mesh.shape["head"]),
        mesh=mesh,
        in_specs=(
            P("ctx", "head"),
            P("ctx", "head"),
            P("ctx", "head"),
            P("ctx", "head"),
            P("head", "ctx"),
            P("head"),
            P("head"),
            P("head", None),
            P(("ctx", "head"), None),
        ),
        out_specs=(
            P(("ctx", "head"), None),
            P("ctx", "head"),
            P("ctx", "head"),
            P("ctx", "head"),
            P("ctx", "head"),
            P("head", "ctx"),
            P("head"),
            P("head"),
            P("head", None),
        ),
        check_vma=False,
    )
```

```python
from functools import partial

import jax
import jax.numpy as jnp
from jax import lax
from jax.experimental import pallas as pl
from jax.experimental.pallas import tpu as pltpu
from jax.sharding import PartitionSpec as P

P_SIZE = 64
N = 128
CHUNK = 256
PIECE = 128
LAG = 8
LAG_HOP = 6
LAG_SIDE = 7
F32 = jnp.float32
BF16 = jnp.bfloat16
VMEM_LIMIT = 46 * 1024 * 1024
MESH = pl.DeviceIdType.MESH

NN = (((1,), (0,)), ((), ()))
NT = (((1,), (1,)), ((), ()))
TN = (((0,), (0,)), ((), ()))


def mm(a, b, dims=NN):
    return lax.dot_general(a, b, dims, preferred_element_type=F32)


def spread(factor, width):
    rows = factor.shape[0]
    left = lax.broadcasted_iota(jnp.int32, (rows, 128), 1) < P_SIZE
    pairs = []
    for k in range(width // 128):
        a = jnp.broadcast_to(factor[:, 2 * k : 2 * k + 1], (rows, 128))
        b = jnp.broadcast_to(factor[:, 2 * k + 1 : 2 * k + 2], (rows, 128))
        pairs.append(jnp.where(left, a, b))
    return jnp.concatenate(pairs, axis=1)


def cumulated(log_row):
    heads, length = log_row.shape
    hi = log_row.astype(BF16).astype(F32)
    rest = log_row - hi
    mid = rest.astype(BF16).astype(F32)
    low = rest - mid
    parts = jnp.concatenate([hi, mid, low, jnp.zeros_like(hi)], axis=0).astype(BF16)
    upper = (
        lax.broadcasted_iota(jnp.int32, (length, length), 0)
        <= lax.broadcasted_iota(jnp.int32, (length, length), 1)
    )
    sums = mm(parts, jnp.where(upper, 1.0, 0.0).astype(BF16))
    row = sums[0:heads] + sums[heads : 2 * heads] + sums[2 * heads : 3 * heads]
    col = jnp.transpose(jnp.concatenate([row] * (128 // heads), axis=0))
    return row, col


def layer_kernel(
    sizes,
    x_hbm, z_hbm, b_hbm, c_hbm, log_hbm, w_hbm, og_hbm, skip_s, gain_ref,
    layer_v, signal_v, gate_v, map_v, read_v, decay_v, gain_out, skip_out, fin,
    x_v, z_v, b_v, c_v, log_v, w_v, rows_v,
    row_t, col_t, start_t, close_t,
    own_s, own_f, got_s, got_f, turned, arriving,
    core_v, entry_v, normed_v, other_n, trans_n,
    dy_v, dn_v, skip_ref,
    out_flow, own_l, got_l, turned_l, arriving_l, sums_v, got_p,
    layer_part, layer_got,
    stage, from_left, from_right,
    in_sem, own_row_sem,
    row_send, row_recv, ex_send, ex_recv, be_send, be_recv, norm_send, norm_recv, lay_send, lay_recv,
    line_send, left_recv, right_recv, fin_left, fin_right, fin_recv, side_send, side_recv,
):
    n, nh, tokens, groups, width, model = sizes
    spans = tokens // CHUNK
    half_w = width // 2
    heads = width // P_SIZE
    block = og_hbm.shape[0]
    share = 16
    holders = N // share
    stride = max(1, n // holders)
    line = n // 2
    root = (line - 1) // 2
    cols = model // PIECE
    halves = model // 2

    me = lax.axis_index("ctx")
    hd = lax.axis_index("head")
    side = lax.rem(me, 2)
    other = 1 - side
    pair = me + 1 - 2 * side
    at_line = me // 2
    core = lax.rem(hd, 2)
    sibling = hd + 1 - 2 * core

    def wrap(i, size):
        return lax.rem(i + size, size)

    def when(cond, fn):
        if cond is True:
            fn()
        else:
            pl.when(cond)(fn)

    inputs = [
        (log_hbm, log_v), (b_hbm, b_v), (x_hbm, x_v), (c_hbm, c_v), (z_hbm, z_v), (w_hbm, w_v),
    ]
    loads = [pltpu.make_async_copy(a, b, in_sem.at[i]) for i, (a, b) in enumerate(inputs)]
    for load in loads[:3]:
        load.start()

    def row_at(which, head, q):
        at = pl.ds(pl.multiple_of(head * block, 16), block)
        return rows_v.at[which, at, pl.ds(q * halves, halves)]

    own_rows = [
        pltpu.make_async_copy(
            og_hbm.at[:, pl.ds(q * halves, halves)], row_at(side, hd, q), own_row_sem.at[q]
        )
        for q in range(2)
    ]
    for copy in own_rows:
        copy.start()

    barrier = pltpu.get_barrier_semaphore()
    for k in range(1, n):
        pl.semaphore_signal(
            barrier, inc=1, device_id={"ctx": wrap(me + k, n)}, device_id_type=MESH
        )
    for k in range(1, nh):
        pl.semaphore_signal(
            barrier, inc=1, device_id={"head": wrap(hd + k, nh)}, device_id_type=MESH
        )
    pl.semaphore_wait(barrier, n - 1 + nh - 1)

    chips = nh // 2

    def row_copy(q, kind, k):
        x_next = wrap(hd + 2 * k, nh)
        x_from = wrap(hd - 2 * k, nh)
        if kind in ("x", "sib", "side"):
            src = og_hbm.at[:, pl.ds(q * halves, halves)]
            dst = row_at(side, hd, q)
        elif kind == "x_sib":
            src = dst = row_at(side, x_from, q)
        elif kind in ("side_sib", "side_x"):
            src = dst = row_at(other, hd, q)
        else:
            src = dst = row_at(other, x_from, q)
        if kind in ("x", "side_x"):
            target = {"head": x_next}
        elif kind == "side":
            target = {"ctx": pair}
        else:
            target = {"head": sibling}
        i = {"sib": 0, "side": 1, "side_sib": 2}.get(kind)
        if i is None:
            i = 3 + {"x": 0, "x_sib": 1, "side_x": 2, "side_x_sib": 3}[kind] * (chips - 1) + k - 1
        return pltpu.make_async_remote_copy(
            src, dst, row_send.at[q, i], row_recv.at[q, i], device_id=target, device_id_type=MESH
        )

    away = range(1, chips)
    row_all = [("sib", 0), ("side", 0), ("side_sib", 0)]
    row_all += [(kind, k) for kind in ("x", "x_sib", "side_x", "side_x_sib") for k in away]
    for q in range(2):
        for k in away:
            row_copy(q, "x", k).start()
        if q == 0:
            row_copy(q, "side", 0).start()
        row_copy(q, "sib", 0).start()

    def rows_side(q):
        row_copy(q, "side", 0).start()

    def rows_relay(q):
        row_copy(q, "side", 0).wait_recv()
        for k in away:
            row_copy(q, "side_x", k).start()
        row_copy(q, "side_sib", 0).start()

    def rows_near(q):
        for k in away:
            row_copy(q, "x", k).wait_recv()
            row_copy(q, "x_sib", k).start()

    def rows_end(q):
        for k in away:
            row_copy(q, "side_x", k).wait_recv()
            row_copy(q, "side_x_sib", k).start()

    def rows_own(q):
        row_copy(q, "sib", 0).wait_recv()
        own_rows[q].wait()
        for k in away:
            row_copy(q, "x_sib", k).wait_recv()

    def rows_last(q):
        row_copy(q, "side_sib", 0).wait_recv()
        for k in away:
            row_copy(q, "side_x_sib", k).wait_recv()

    is_holder = True if stride == 1 else lax.rem(me, stride) == 0
    my_share = pl.multiple_of(me // stride * share, share)

    def holds(i):
        return True if stride == 1 else lax.rem(i, stride) == 0

    def exchange(base, g, state, got, result, into):
        def first(k):
            to = wrap(me + k, n)
            part = pl.ds(pl.multiple_of(to // stride * share, share), share)
            return pltpu.make_async_remote_copy(
                state.at[g, part, :], got.at[me, g],
                ex_send.at[base + 2 * g, k], ex_recv.at[base + 2 * g, k],
                device_id={"ctx": to}, device_id_type=MESH,
            )

        def second(k):
            to = wrap(me + k, n)
            return pltpu.make_async_remote_copy(
                result.at[to, g], into.at[g, pl.ds(my_share, share), :],
                ex_send.at[base + 2 * g + 1, k], ex_recv.at[base + 2 * g + 1, k],
                device_id={"ctx": to}, device_id_type=MESH,
            )

        return first, second

    def beside(i, src, dst, k):
        return pltpu.make_async_remote_copy(
            src, dst, be_send.at[i, k], be_recv.at[i, k],
            device_id={"ctx": wrap(me + k, n)}, device_id_type=MESH,
        )

    def fade_copy(g, k):
        return beside(g, own_f.at[g], got_f.at[me, g], k)

    def sums_copy(k):
        return beside(groups, sums_v, got_p.at[me], k)

    def send_shares(copies, g, state, got, fades):
        for k in range(1, n):
            def _(k=k):
                if fades:
                    fade_copy(g, k).start()
                copies[0](k).start()
            when(holds(wrap(me + k, n)), _)

        def _():
            got[pl.ds(me, 1), g] = state[g, pl.ds(my_share, share), :][None]
            if fades:
                got_f[pl.ds(me, 1), g] = own_f[g][None]
        when(is_holder, _)

    def carry_shares(copies, g, got, result, into, reverse):
        first, second = copies

        def _():
            for k in range(1, n):
                if not reverse:
                    fade_copy(g, k).wait_recv()
                first(k).wait_recv()
            carried = jnp.zeros((share, width), F32)
            for d in reversed(range(n)) if reverse else range(n):
                result[d, g] = carried.astype(BF16)
                carried = got_f[d, g] * carried + got[d, g].astype(F32)
            for k in range(1, n):
                second(k).start()
            into[g, pl.ds(my_share, share), :] = result[me, g]
        when(is_holder, _)

    def take_shares(copies):
        for k in range(1, n):
            def _(k=k):
                copies[1](k).wait_recv()
            when(holds(wrap(me - k, n)), _)

    def drain_shares(copies, g, fades):
        for k in range(1, n):
            def _(k=k):
                if fades:
                    fade_copy(g, k).wait_send()
                copies[0](k).wait_send()
            when(holds(wrap(me + k, n)), _)
            def _(k=k):
                copies[1](k).wait_send()
            when(is_holder, _)

    def at(c):
        return slice(c * CHUNK, (c + 1) * CHUNK)

    def wide(g):
        return slice(g * width, (g + 1) * width)

    def narrow(g):
        return slice(g * N, (g + 1) * N)

    left = lax.broadcasted_iota(jnp.int32, (CHUNK, 128), 1) < P_SIZE

    def local_state(g):
        state = jnp.zeros((N, width), F32)
        decay = jnp.ones((1, width), F32)
        for c in range(spans):
            row, col = cumulated(log_v[g * heads : (g + 1) * heads, at(c)])
            i = g * spans + c
            row_t[i] = row
            col_t[i] = col
            col = col[:, :heads]
            from_start = spread(jnp.exp(col), width)
            to_closing = spread(jnp.exp(col[-1:, :] - col), width)
            start_t[i] = from_start
            close_t[i] = to_closing
            span = from_start[-1:, :]
            scaled = (x_v[at(c), wide(g)].astype(F32) * to_closing).astype(BF16)
            state = state * span + mm(b_v[at(c), narrow(g)], scaled, TN)
            decay = decay * span
        own_s[g] = state.astype(BF16)
        own_f[g] = decay

    def intra(g, c):
        i = g * spans + c
        row, col = row_t[i], col_t[i]
        lower = (
            lax.broadcasted_iota(jnp.int32, (CHUNK, CHUNK), 0)
            >= lax.broadcasted_iota(jnp.int32, (CHUNK, CHUNK), 1)
        )
        x = x_v[at(c), wide(g)]
        inner = mm(c_v[at(c), narrow(g)], b_v[at(c), narrow(g)], NT)
        for k in range(width // 128):
            two = x[:, 128 * k : 128 * k + 128]
            parts = []
            for h in (2 * k, 2 * k + 1):
                gap = jnp.where(lower, col[:, h : h + 1] - row[h : h + 1, :], -1e30)
                parts.append(mm((jnp.exp(gap) * inner).astype(BF16), two))
            lanes = slice(g * width + 128 * k, g * width + 128 * k + 128)
            core_v[at(c), lanes] = jnp.where(left, parts[0], parts[1])

    def norm_copy(g):
        return pltpu.make_async_remote_copy(
            normed_v.at[g, other], other_n.at[g], norm_send.at[g], norm_recv.at[g],
            device_id={"ctx": pair}, device_id_type=MESH,
        )

    def forward(g):
        state = arriving[g].astype(F32)
        for c in range(spans):
            i = g * spans + c
            entry = state.astype(BF16)
            entry_v[i] = entry
            xf = x_v[at(c), wide(g)].astype(F32)
            from_start = start_t[i]
            core_now = core_v[at(c), wide(g)] + from_start * mm(c_v[at(c), narrow(g)], entry)
            core_v[at(c), wide(g)] = core_now
            y = core_now + skip_ref[:, wide(g)] * xf
            z = z_v[at(c), wide(g)].astype(F32)
            gated = y * (z * jax.nn.sigmoid(z))
            inv = lax.rsqrt(jnp.mean(gated * gated, axis=1, keepdims=True) + 1e-05)
            normed = (gated * inv * gain_ref[:, wide(g)]).astype(BF16)
            normed_v[g, 0, at(c), :] = normed[:, :half_w]
            normed_v[g, 1, at(c), :] = normed[:, half_w:]
            if c < spans - 1:
                scaled = (xf * close_t[i]).astype(BF16)
                state = state * from_start[-1:, :] + mm(b_v[at(c), narrow(g)], scaled, TN)
        norm_copy(g).start()
        trans_n[g, :, pl.ds(pl.multiple_of(side * tokens, CHUNK), tokens)] = jnp.transpose(
            normed_v[g, side]
        )

    def dnormed(g, c):
        dn_v[...] = mm(rows_v[side, at(c), :], w_v[wide(g), :], NT).astype(BF16)

    def middle(g, c):
        i = g * spans + c
        from_start = start_t[i]
        gain = gain_ref[:, wide(g)]
        dn = dn_v[...].astype(F32)
        xf = x_v[at(c), wide(g)].astype(F32)
        z = z_v[at(c), wide(g)].astype(F32)
        y = core_v[at(c), wide(g)] + skip_ref[:, wide(g)] * xf
        s = jax.nn.sigmoid(z)
        silu = z * s
        gated = y * silu
        inv = lax.rsqrt(jnp.mean(gated * gated, axis=1, keepdims=True) + 1e-05)
        gain_sum = jnp.sum(dn * gated * inv, axis=0, keepdims=True)
        scaled = gain * dn
        mean = jnp.mean(scaled * gated, axis=1, keepdims=True)
        dgated = inv * scaled - gated * (inv * inv * inv * mean)
        gate_v[at(c), wide(g)] = dgated * y * s * (1.0 + z * (1.0 - s))
        dy = dgated * silu
        dy_v[at(c), wide(g)] = dy
        skip_sum = jnp.sum(dy * xf, axis=0, keepdims=True)
        flow = mm(c_v[at(c), narrow(g)], (dy * from_start).astype(BF16), TN)
        if c == spans - 1:
            sums_v[g : g + 1, :] = gain_sum
            sums_v[groups + g : groups + g + 1, :] = skip_sum
            out_flow[g] = flow
        else:
            sums_v[g : g + 1, :] += gain_sum
            sums_v[groups + g : groups + g + 1, :] += skip_sum
            out_flow[g] = out_flow[g] * from_start[-1:, :] + flow
        if c == 0:
            own_l[g] = out_flow[g].astype(BF16)

    def layer_terms(j):
        cut = slice(j * 512, (j + 1) * 512)
        total = jnp.zeros((tokens, 512), F32)
        for g in range(groups):
            both = jnp.concatenate([normed_v[g, 0], normed_v[g, 1]], axis=1)
            total += mm(both, w_v[wide(g), cut])
        layer_part[:, cut] = total.astype(BF16)

    def layer_copy(k):
        to = wrap(hd + k, nh)
        return pltpu.make_async_remote_copy(
            layer_part.at[pl.ds(pl.multiple_of(to * block, 16), block), :], layer_got.at[k - 1],
            lay_send.at[k - 1], lay_recv.at[k - 1], device_id={"head": to}, device_id_type=MESH,
        )

    def layer_sum():
        total = layer_part[pl.ds(pl.multiple_of(hd * block, 16), block), :].astype(F32)
        for k in range(1, nh):
            layer_copy(k).wait_recv()
            total += layer_got[k - 1].astype(F32)
        layer_v[...] = total.astype(BF16)

    def back_inner(g, c):
        i = g * spans + c
        row, col = row_t[i], col_t[i]
        upper = (
            lax.broadcasted_iota(jnp.int32, (CHUNK, CHUNK), 0)
            <= lax.broadcasted_iota(jnp.int32, (CHUNK, CHUNK), 1)
        )
        x = x_v[at(c), wide(g)]
        xf = x.astype(F32)
        dyf = dy_v[at(c), wide(g)]
        dy = dyf.astype(BF16)
        bm, cm = b_v[at(c), narrow(g)], c_v[at(c), narrow(g)]
        inner = mm(bm, cm, NT)
        pair_sum = jnp.zeros((CHUNK, CHUNK), F32)
        for k in range(width // 128):
            cut = slice(128 * k, 128 * k + 128)
            x_two, dy_two = xf[:, cut], dy[:, cut]
            parts = []
            for h, lanes in ((2 * k, left), (2 * k + 1, ~left)):
                gap = jnp.where(upper, row[h : h + 1, :] - col[:, h : h + 1], -1e30)
                fade = jnp.exp(gap)
                parts.append(mm((fade * inner).astype(BF16), dy_two))
                one = jnp.where(lanes, x_two, 0.0).astype(BF16)
                pair_sum += mm(one, dy_two, NT) * fade
            lanes = slice(g * width + 128 * k, g * width + 128 * k + 128)
            signal_v[at(c), lanes] = jnp.where(left, parts[0], parts[1])
        pair_sum = pair_sum.astype(BF16)
        map_v[at(c), narrow(g)] = mm(pair_sum, cm)
        dy_start = (dyf * start_t[i]).astype(BF16)
        read_v[at(c), narrow(g)] = mm(pair_sum, bm, TN) + mm(dy_start, entry_v[i], NT)

    def back_outer(g):
        own = (
            lax.broadcasted_iota(jnp.int32, (heads, width), 1) // P_SIZE
            == lax.broadcasted_iota(jnp.int32, (heads, width), 0)
        )
        own = jnp.where(own, 1.0, 0.0).astype(BF16)
        flow = arriving_l[g].astype(F32)
        for c in reversed(range(spans)):
            i = g * spans + c
            out = flow.astype(BF16)
            xf = x_v[at(c), wide(g)].astype(F32)
            dyf = dy_v[at(c), wide(g)]
            to_closing = close_t[i]
            core_grad = signal_v[at(c), wide(g)] + to_closing * mm(b_v[at(c), narrow(g)], out)
            signal_v[at(c), wide(g)] = core_grad + skip_ref[:, wide(g)] * dyf
            map_v[at(c), narrow(g)] += mm((xf * to_closing).astype(BF16), out, NT)
            slope = dyf * core_v[at(c), wide(g)] - xf * core_grad
            hi = slope.astype(BF16)
            low = (slope - hi.astype(F32)).astype(BF16)
            decay_v[g * heads : (g + 1) * heads, at(c)] = mm(own, hi, NT) + mm(own, low, NT)
            if c > 0:
                from_start = start_t[i]
                dy_start = (dyf * from_start).astype(BF16)
                flow = flow * from_start[-1:, :] + mm(c_v[at(c), narrow(g)], dy_start, TN)

    pieces = [(g, j) for g in range(groups) for j in range(cols)]
    below, above, here = at_line < root, at_line > root, at_line == root
    first_end, last_end = at_line == 0, at_line == line - 1
    lower_id, upper_id = wrap(me - 2, n), wrap(me + 2, n)

    def remote(src, dst, send, recv, to):
        return pltpu.make_async_remote_copy(
            src, dst, send, recv, device_id={"ctx": to}, device_id_type=MESH
        )

    def term_up(i):
        return remote(stage.at[i], from_left.at[i], line_send.at[i], left_recv.at[i], upper_id)

    def term_down(i):
        return remote(stage.at[i], from_right.at[i], line_send.at[i], right_recv.at[i], lower_id)

    def fin_at(i, which):
        return fin.at[i // cols, which, lax.rem(i, cols)]

    def fin_down(i):
        return remote(fin_at(i, side), fin_at(i, side), fin_left.at[i], fin_recv.at[i], lower_id)

    def fin_up(i):
        return remote(fin_at(i, side), fin_at(i, side), fin_right.at[i], fin_recv.at[i], upper_id)

    def fin_side(i):
        return remote(fin_at(i, side), fin_at(i, side), side_send.at[i], side_recv.at[i], pair)

    def fin_side_in(i):
        return remote(fin_at(i, other), fin_at(i, other), side_send.at[i], side_recv.at[i], pair)

    def reduce_piece(i):
        g, j = pieces[i]
        if j == 0:
            norm_copy(g).wait_recv()
            trans_n[g, :, pl.ds(pl.multiple_of(other * tokens, CHUNK), tokens)] = jnp.transpose(
                other_n[g]
            )
        cut = slice(j * PIECE, (j + 1) * PIECE)
        own = mm(trans_n[g, :, :tokens], rows_v[0, :, cut])
        own += mm(trans_n[g, :, tokens:], rows_v[1, :, cut])

        @pl.when(below)
        def _():
            @pl.when(first_end)
            def _():
                stage[i] = own.astype(BF16)

            @pl.when(jnp.logical_not(first_end))
            def _():
                term_up(i).wait_recv()
                stage[i] = (own + from_left[i].astype(F32)).astype(BF16)

            term_up(i).start()

        @pl.when(above)
        def _():
            @pl.when(last_end)
            def _():
                stage[i] = own.astype(BF16)

            @pl.when(jnp.logical_not(last_end))
            def _():
                term_down(i).wait_recv()
                stage[i] = (own + from_right[i].astype(F32)).astype(BF16)

            term_down(i).start()

        @pl.when(here)
        def _():
            total = own
            if root > 0:
                term_up(i).wait_recv()
                total += from_left[i].astype(F32)
            if root < line - 1:
                term_down(i).wait_recv()
                total += from_right[i].astype(F32)
            fin[g, pl.ds(side, 1), j] = total.astype(BF16)[None]
            if root > 0:
                fin_down(i).start()
            if root < line - 1:
                fin_up(i).start()
            fin_side(i).start()

    def pass_on(i):
        @pl.when(jnp.logical_not(here))
        def _():
            fin_up(i).wait_recv()

            @pl.when(jnp.logical_and(below, jnp.logical_not(first_end)))
            def _():
                fin_down(i).start()

            @pl.when(jnp.logical_and(above, jnp.logical_not(last_end)))
            def _():
                fin_up(i).start()

            fin_side(i).start()

    def take_side(i):
        fin_side_in(i).wait_recv()

    def drain_piece(i):
        @pl.when(jnp.logical_not(here))
        def _():
            term_up(i).wait_send()

        goes_down = jnp.logical_or(
            jnp.logical_and(here, jnp.logical_not(first_end)),
            jnp.logical_and(below, jnp.logical_not(first_end)),
        )
        goes_up = jnp.logical_or(
            jnp.logical_and(here, jnp.logical_not(last_end)),
            jnp.logical_and(above, jnp.logical_not(last_end)),
        )

        @pl.when(goes_down)
        def _():
            fin_down(i).wait_send()

        @pl.when(goes_up)
        def _():
            fin_up(i).wait_send()

        fin_side(i).wait_send()

    ex_f = [exchange(0, g, own_s, got_s, turned, arriving) for g in range(groups)]
    ex_b = [exchange(2 * groups, g, own_l, got_l, turned_l, arriving_l) for g in range(groups)]

    ones = lax.broadcasted_iota(jnp.int32, (1, 128), 1) < P_SIZE
    for k in range(groups * width // 128):
        skip_ref[:, 128 * k : 128 * k + 128] = jnp.where(ones, skip_s[2 * k], skip_s[2 * k + 1])

    for i in (0, 1, 2):
        loads[i].wait()
    for load in loads[3:]:
        load.start()
    for g in range(groups):
        local_state(g)
        send_shares(ex_f[g], g, own_s, got_s, True)
    loads[3].wait()
    todo = [(g, c) for g in range(groups) for c in range(spans)]
    intra(*todo[0])
    for g in range(groups):
        carry_shares(ex_f[g], g, got_s, turned, arriving, False)
        if g == 0:
            rows_near(0)
            rows_relay(0)
        intra(*todo[1 + g])
    loads[4].wait()
    take_shares(ex_f[0])
    forward(0)
    rows_side(1)
    for one in todo[1 + groups :]:
        intra(*one)
    rows_end(0)
    for g in range(1, groups):
        take_shares(ex_f[g])
        forward(g)
    rows_own(0)
    rows_last(0)
    rows_near(1)
    loads[5].wait()

    def rows_full():
        rows_end(1)
        rows_last(1)

    def start_layer():
        for k in range(1, nh):
            layer_copy(k).start()

    def later_send(g):
        send_shares(ex_b[g], g, own_l, got_l, False)

    def sums_send():
        for k in range(1, n):
            sums_copy(k).start()
        got_p[pl.ds(me, 1)] = sums_v[...][None]

    def later_carry(g):
        carry_shares(ex_b[g], g, got_l, turned_l, arriving_l, True)

    def params_sum():
        for k in range(1, n):
            sums_copy(k).wait_recv()
        total = jnp.zeros((2 * groups, width), F32)
        for d in range(n):
            total += got_p[d]
        lane = lax.broadcasted_iota(jnp.int32, (1, width), 1) // P_SIZE
        spot = lax.broadcasted_iota(jnp.int32, (1, groups * heads), 1)
        found = jnp.zeros((1, groups * heads), F32)
        for g in range(groups):
            gain_out[:, wide(g)] = total[g : g + 1]
            row = total[groups + g : groups + g + 1]
            for h in range(heads):
                head = jnp.sum(jnp.where(lane == h, row, 0.0), axis=1, keepdims=True)
                found = jnp.where(spot == g * heads + h, head, found)
        skip_out[...] = found

    items = [(0.6, partial(layer_terms, j)) for j in range(model // 512)]
    items += [(0.1, start_layer)]
    for g in range(groups):
        for c in reversed(range(spans)):
            items += [(0.8, partial(dnormed, g, c)), (2.2, partial(middle, g, c))]
        items += [(0.4, partial(later_send, g))]
    items += [(0.2, sums_send)]
    inner_items = [(2.2, partial(back_inner, g, c)) for g in range(groups) for c in range(spans)]
    items += inner_items[: len(inner_items) // 2]
    items += [(0.5, partial(later_carry, g)) for g in range(groups)]
    items += inner_items[len(inner_items) // 2 :]
    for g in range(groups):
        items += [(0.2, partial(take_shares, ex_b[g])), (1.2, partial(back_outer, g))]
    items += [(0.5, params_sum), (0.5, layer_sum)]

    count = len(pieces)
    lag = jnp.where(here, 0, LAG + LAG_HOP * (jnp.abs(at_line - root) - 1))
    max_lag = LAG + LAG_HOP * (max(root, line - 1 - root) - 1)
    ticks = count + max_lag + LAG_SIDE
    busy = count + max_lag // 2
    per_tick = sum(share for share, _ in items) / busy
    first_full = cols // 2
    spent = 0.0
    for t in range(ticks):
        if t == first_full // 4:
            rows_relay(1)
        if t == first_full:
            rows_full()
        if t < count:
            reduce_piece(t)

        @pl.when(jnp.logical_and(t - lag >= 0, t - lag < count))
        def _():
            pass_on(t - lag)

        late = t - lag - LAG_SIDE

        @pl.when(jnp.logical_and(late >= 0, late < count))
        def _():
            take_side(late)

        if t == 0:
            rows_own(1)
        while items and (spent < (t + 1) * per_tick or t + 1 >= busy):
            spent += items[0][0]
            items.pop(0)[1]()

    for q in range(2):
        for kind, k in row_all:
            row_copy(q, kind, k).wait_send()
    for g in range(groups):
        drain_shares(ex_f[g], g, True)
        drain_shares(ex_b[g], g, False)
    for k in range(1, n):
        sums_copy(k).wait_send()
    for g in range(groups):
        norm_copy(g).wait_send()
    for k in range(1, nh):
        layer_copy(k).wait_send()
    for i in range(count):
        drain_piece(jnp.int32(i))


def finish_kernel(
    layer_in, signal_in, gate_in, map_in, read_in, decay_in, gain_in, skip_in, weight_in,
    layer_out, signal_out, gate_out, map_out, read_out, decay_out, gain_out, skip_out, weight_out,
    wide_v, sem, weight_sem,
):
    groups, sides, cols, half_w, _ = weight_in.shape
    pairs = [
        (signal_in, signal_out), (gate_in, gate_out), (map_in, map_out), (read_in, read_out),
        (layer_in, layer_out), (decay_in, decay_out), (gain_in, gain_out), (skip_in, skip_out),
    ]
    copies = [pltpu.make_async_copy(a, b, sem.at[i]) for i, (a, b) in enumerate(pairs)]
    for copy in copies:
        copy.start()
    for g in range(groups):
        for s in range(sides):
            i = g * sides + s
            for j in range(cols):
                wide_v[i, :, j * PIECE : (j + 1) * PIECE] = weight_in[g, s, j].astype(F32)
            copy = pltpu.make_async_copy(
                wide_v.at[i], weight_out.at[pl.ds(i * half_w, half_w), :], weight_sem.at[i]
            )
            copy.start()
            copies.append(copy)
    for copy in copies:
        copy.wait()


def on_device(
    n, nh,
    signal, gate_input, input_map, readout, log_decay, skip_gain, norm_gain, out_weight, out_grad,
):
    tokens, features = signal.shape
    heads = log_decay.shape[0]
    groups = input_map.shape[1] // N
    width = features // groups
    model = out_weight.shape[1]
    block = out_grad.shape[0]
    spans = tokens // CHUNK
    cols = model // PIECE
    count = groups * cols
    half_w = width // 2
    chips = nh // 2
    sds = jax.ShapeDtypeStruct
    vm = pltpu.VMEM
    dma = pltpu.SemaphoreType.DMA

    gain = norm_gain.reshape(1, features)
    hbm = pl.BlockSpec(memory_space=pl.ANY)
    near = pl.BlockSpec(memory_space=pltpu.VMEM)
    sizes = (n, nh, tokens, groups, width, model)
    kinds = 3 + 4 * (chips - 1)
    all_spans = groups * spans
    results = [
        ((block, model), BF16),
        ((tokens, features), F32),
        ((tokens, features), F32),
        ((tokens, groups * N), F32),
        ((tokens, groups * N), F32),
        ((heads, tokens), F32),
        ((1, features), F32),
        ((1, heads), F32),
        ((groups, 2, cols, half_w, PIECE), BF16),
    ]
    held = pl.pallas_call(
        partial(layer_kernel, sizes),
        in_specs=[hbm] * 7 + [pl.BlockSpec(memory_space=pltpu.SMEM), near],
        out_specs=[near] * 9,
        out_shape=[pltpu.VMEM(shape, dtype) for shape, dtype in results],
        scratch_shapes=[
            vm((tokens, features), BF16), vm((tokens, features), BF16),
            vm((tokens, groups * N), BF16), vm((tokens, groups * N), BF16),
            vm((heads, tokens), F32), vm((features, model), BF16), vm((2, tokens, model), BF16),
            vm((all_spans, heads // groups, CHUNK), F32), vm((all_spans, CHUNK, 128), F32),
            vm((all_spans, CHUNK, width), F32), vm((all_spans, CHUNK, width), F32),
            vm((groups, N, width), BF16), vm((groups, 1, width), F32),
            vm((n, groups, 16, width), BF16), vm((n, groups, 1, width), F32),
            vm((n, groups, 16, width), BF16), vm((groups, N, width), BF16),
            vm((tokens, features), F32), vm((all_spans, N, width), BF16),
            vm((groups, 2, tokens, half_w), BF16), vm((groups, tokens, half_w), BF16),
            vm((groups, half_w, 2 * tokens), BF16),
            vm((tokens, features), F32), vm((CHUNK, width), BF16), vm((1, features), F32),
            vm((groups, N, width), F32), vm((groups, N, width), BF16),
            vm((n, groups, 16, width), BF16), vm((n, groups, 16, width), BF16),
            vm((groups, N, width), BF16),
            vm((2 * groups, width), F32), vm((n, 2 * groups, width), F32),
            vm((tokens, model), BF16), vm((nh - 1, block, model), BF16),
            vm((count, half_w, PIECE), BF16), vm((count, half_w, PIECE), BF16),
            vm((count, half_w, PIECE), BF16),
            dma((6,)), dma((2,)),
            dma((2, kinds)), dma((2, kinds)), dma((4 * groups, n)), dma((4 * groups, n)),
            dma((groups + 1, n)), dma((groups + 1, n)),
            dma((groups,)), dma((groups,)), dma((nh - 1,)), dma((nh - 1,)),
            dma((count,)), dma((count,)), dma((count,)), dma((count,)), dma((count,)), dma((count,)),
            dma((count,)), dma((count,)),
        ],
        compiler_params=pltpu.CompilerParams(
            collective_id=0, has_side_effects=True, vmem_limit_bytes=VMEM_LIMIT
        ),
        name="layer",
    )(signal, gate_input, input_map, readout, log_decay, out_weight, out_grad, skip_gain, gain)

    results[-1] = ((features, model), F32)
    outs = pl.pallas_call(
        finish_kernel,
        in_specs=[near] * 9,
        out_specs=[hbm] * 9,
        out_shape=[sds(shape, dtype) for shape, dtype in results],
        scratch_shapes=[vm((2 * groups, half_w, model), F32), dma((8,)), dma((2 * groups,))],
        compiler_params=pltpu.CompilerParams(vmem_limit_bytes=24 * 1024 * 1024),
        name="finish",
    )(*held)
    layer_out, signal_grad, gate_grad, map_grad, read_grad, decay_grad, gain, skip, weight = outs
    return (
        layer_out, signal_grad, gate_grad, map_grad, read_grad, decay_grad,
        skip.reshape(heads), gain.reshape(features), weight,
    )


def solution(mesh):
    return jax.shard_map(
        partial(on_device, mesh.shape["ctx"], mesh.shape["head"]),
        mesh=mesh,
        in_specs=(
            P("ctx", "head"),
            P("ctx", "head"),
            P("ctx", "head"),
            P("ctx", "head"),
            P("head", "ctx"),
            P("head"),
            P("head"),
            P("head", None),
            P(("ctx", "head"), None),
        ),
        out_specs=(
            P(("ctx", "head"), None),
            P("ctx", "head"),
            P("ctx", "head"),
            P("ctx", "head"),
            P("ctx", "head"),
            P("head", "ctx"),
            P("head"),
            P("head"),
            P("head", None),
        ),
        check_vma=False,
    )
```
